256 devices in a mesh: dom: 32 (over z, x_hi, core), frame: 8 (over x_lo, y).
Axes of the slice: x: 4 (x_hi: 2, x_lo: 2; x = x_hi * 2 + x_lo), y: 4, z: 8, core: 2. Of those that a mesh axis runs over, the one named last changes fastest.
Arguments:
- features: bfloat16 [4096, 512], P('dom'), may hold values from -6 to 6
- positions: bfloat16 [3, 4096], P(None, 'dom'), may hold values from 0 to 4
- neighbours: int32 [4096, 128], P('dom'), may hold values from 0 to 255, as said below
- counts: int32 [4096], P('dom'), may hold values from 1 to 128, as said below
- send_rows: int32 [32, 2, 64], P('dom'), may hold values from 0 to 127
- frames: float32 [8, 3, 3], P('frame')
- w_edge: float32 [9, 512], replicated, may hold values from -2 to 2
- b_edge: float32 [512], replicated, may hold values from -4 to 4
- w_message: bfloat16 [512, 512], replicated, may hold values from -0.25 to 0.25
- w_update: bfloat16 [512, 512], replicated, may hold values from -0.25 to 0.25
- w_readout: bfloat16 [512, 512], replicated, may hold values from -0.25 to 0.25
- w_heads: bfloat16 [512, 4], replicated, may hold values from -0.25 to 0.25
Outputs:
- predictions: float32 [4, 4096], P(None, 'dom')
The draws below stay inside these ranges and needn't reach their ends.
Inputs may be any that keep to these rules, and one draw needn't show every extreme that they name: `counts`: each domain has its own largest count, one of 32, 64, 96 or 128, reached by one of its atoms; some domain reaches 128. `neighbours`: order a domain's table as the 64 rows from the domain below, its own 128 atoms, then the 64 rows from the domain above; every slot of an atom in aligned block b of 16 atoms of its domain names a row at positions (b * 128) // max(7, 1) to that plus 128 - 1 of this order.
All inputs are finite; a program needn't handle non-finite values.
Results may differ from the reference program's by a relative error of at most 0.0049.
Values may be sent and summed in bfloat16 or wider, within the bound.
No kernel may reach another device: no remote copies, remote signals or barrier semaphores. Data moves between devices by JAX's collectives and lax.ppermute only.
A program may use at most 64 MiB of HBM per device.

```python
import math
import jax
import jax.numpy as jnp
from jax import lax

W = 512
RBF = 6
NEIGH = 128
WINDOW = 128
ATOMS_DEV = 128
CAP = 64
ATOMS = 4096
N_DOM = 32
N_FRAME = 8


def draw_neighbours(key, part):
    table_rows = ATOMS_DEV + 2 * CAP
    block_total = ATOMS_DEV // 16
    span_rows = table_rows - WINDOW
    denom = max(block_total - 1, 1)
    starts = jnp.arange(block_total, dtype=jnp.int32) * span_rows // denom
    offsets = jax.random.randint(jax.random.fold_in(key, 31), (N_DOM, block_total, 16, NEIGH), 0, WINDOW)
    placed = starts[None, :, None, None] + offsets
    placed = placed.at[:, block_total - 1, 0, 0].set(table_rows - 1)
    zero_block = min(CAP * (block_total - 1) // max(span_rows, 1), block_total - 1)
    placed = placed.at[:, zero_block, 0, 1].set(CAP)
    values = jnp.where(placed < CAP, ATOMS_DEV + placed, jnp.where(placed < CAP + ATOMS_DEV, placed - CAP, placed))
    return values.reshape(N_DOM * ATOMS_DEV, NEIGH).astype(jnp.int32)


def draw_counts(key, part):
    key_order = jax.random.fold_in(key, 11)
    key_count = jax.random.fold_in(key, 12)
    key_peak = jax.random.fold_in(key, 13)
    order = jax.random.permutation(key_order, N_DOM)
    density = 1 + order % 4
    density_top = NEIGH * density // 4
    raw_draw = jax.random.randint(key_count, (N_DOM, ATOMS_DEV), 0, 1 << 20)
    drawn = raw_draw % density_top[:, None] + 1
    peak_spot = jax.random.randint(key_peak, (N_DOM, 1), 0, ATOMS_DEV)
    peak_mask = jnp.arange(ATOMS_DEV)[None, :] == peak_spot
    return jnp.where(peak_mask, density_top[:, None], drawn).reshape(-1).astype(jnp.int32)


def draw_frames(key, part):
    key_angle = jax.random.fold_in(key, 21)
    angles = jax.random.uniform(key_angle, (3,), jnp.float32, -math.pi, math.pi)
    cosines = jnp.cos(angles)
    sines = jnp.sin(angles)
    basis = jnp.stack([cosines[1] * cosines[0], cosines[0] * sines[1] * sines[2] - sines[0] * cosines[2], cosines[0] * sines[1] * cosines[2] + sines[0] * sines[2], cosines[1] * sines[0], sines[0] * sines[1] * sines[2] + cosines[0] * cosines[2], sines[0] * sines[1] * cosines[2] - cosines[0] * sines[2], -sines[1], cosines[1] * sines[2], cosines[1] * cosines[2]]).reshape(3, 3)
    flips = jnp.arange(N_FRAME, dtype=jnp.int32)[:, None] >> jnp.arange(3, dtype=jnp.int32)[None, :] & 1
    signs = 1.0 - 2.0 * flips.astype(jnp.float32)
    return (signs[:, :, None] * basis[None, :, :]).astype(jnp.float32)


def set_ends(entries, own_key, low, top_value):
    spot = [jax.random.randint(jax.random.fold_in(own_key, axis), (), 0, length) for axis, length in enumerate(entries.shape)]
    main_axis = entries.shape.index(max(entries.shape))
    beside = spot[:main_axis] + [(spot[main_axis] + 1) % entries.shape[main_axis]] + spot[main_axis + 1:]
    return entries.at[tuple(spot)].set(low).at[tuple(beside)].set(top_value)


def levels(rng, extent, cuts, low, largest):
    loudness = 1.0
    for position, shards_of in cuts:
        heights = jax.random.uniform(jax.random.fold_in(jax.random.fold_in(rng, 6), position), (shards_of,), jnp.float32, low / len(cuts), largest / len(cuts))
        loudness = loudness * jnp.repeat(jnp.exp(heights), extent[position] // shards_of).reshape((-1,) + (1,) * (len(extent) - 1 - position))
    return loudness


def gaussian(rng, shape, scale, most, shards=(), held_as=jnp.bfloat16):
    values = jax.random.normal(rng, shape, jnp.float32) * scale
    if len(shards) > 0:
        values = levels(rng, shape, shards, -0.22, 0.18) * values
    return jnp.clip(values, min=-most, max=most).astype(held_as)


def setup_inputs(seed: int = 0) -> dict:
    streams_of = jax.random.split(jax.random.key(seed), 13)
    features = gaussian(streams_of[0], (ATOMS, W), 1.0, 6.0, ((0, 32),))
    positions = jnp.clip(4.0 * jax.random.uniform(streams_of[1], (3, ATOMS), jnp.float32) ** levels(streams_of[1], (3, ATOMS), ((1, 32),), -0.2, 0.2), 0.0, 4.0).astype(jnp.bfloat16)
    neighbours = draw_neighbours(jax.random.fold_in(streams_of[12], 71), 0)
    counts = draw_counts(jax.random.fold_in(streams_of[12], 71), 0)
    send_rows = set_ends(jax.random.randint(streams_of[4], (N_DOM, 2, CAP), 0, ATOMS_DEV), jax.random.fold_in(streams_of[4], 1), 0, ATOMS_DEV - 1).astype(jnp.int32)
    frames = draw_frames(jax.random.fold_in(streams_of[12], 71), 0)
    w_edge = gaussian(streams_of[6], (RBF + 3, W), (RBF + 3) ** -0.5, 2.0, (), jnp.float32)
    b_edge = gaussian(streams_of[7], (W,), 1.0, 4.0, (), jnp.float32)
    w_message = gaussian(streams_of[8], (W, W), W ** -0.5, 0.25)
    w_update = gaussian(streams_of[9], (W, W), W ** -0.5, 0.25)
    w_readout = gaussian(streams_of[10], (W, W), W ** -0.5, 0.25)
    w_heads = gaussian(streams_of[11], (W, 4), W ** -0.5, 0.25)
    return dict(features=features, positions=positions, neighbours=neighbours, counts=counts, send_rows=send_rows, frames=frames, w_edge=w_edge, b_edge=b_edge, w_message=w_message, w_update=w_update, w_readout=w_readout, w_heads=w_heads)


message_scale = 0.0884
radial_step = 1.25

def edge_messages(rows_feat, rows_pos, centre_pos, live_mask, rotation, w_edge, b_edge):
    relative = rows_pos - centre_pos[:, None, :]
    frame_vec = jnp.einsum('bkc,ac->bka', relative, rotation, precision=lax.Precision.HIGHEST)
    distance = jnp.sqrt(lax.optimization_barrier(jnp.sum(relative * relative, axis=-1)) + 0.25)
    centres = jnp.arange(w_edge.shape[0] - 3, dtype=jnp.float32) * radial_step
    radial = jnp.exp(-(distance[..., None] - centres) ** 2)
    edge_in = jnp.concatenate([radial, frame_vec], axis=-1)
    preact = jnp.einsum('bki,iw->bkw', edge_in, w_edge, precision=lax.Precision.HIGHEST) + b_edge
    edge_gate = jax.nn.silu(preact) * live_mask[..., None]
    return lax.optimization_barrier(jnp.sum(edge_gate * rows_feat.astype(jnp.float32), axis=1)) * message_scale

def reference(features, positions, neighbours, counts, send_rows, frames, w_edge, b_edge, w_message, w_update, w_readout, w_heads):
    domain_ids = jnp.arange(N_DOM, dtype=jnp.int32)
    lower_src = ((domain_ids - 1) % N_DOM).astype(jnp.int32)
    upper_src = ((domain_ids + 1) % N_DOM).astype(jnp.int32)
    ghost_lower = lower_src[:, None] * ATOMS_DEV + send_rows[lower_src, 1, :].astype(jnp.int32)
    ghost_upper = upper_src[:, None] * ATOMS_DEV + send_rows[upper_src, 0, :].astype(jnp.int32)
    ghost_global = jnp.concatenate([ghost_lower, ghost_upper], axis=1).astype(jnp.int32)
    own_global = domain_ids[:, None] * ATOMS_DEV + jnp.arange(ATOMS_DEV, dtype=jnp.int32)[None, :]
    lookup = jnp.concatenate([own_global, ghost_global], axis=1)
    edge_global = jnp.take_along_axis(lookup, neighbours.reshape(N_DOM, ATOMS_DEV * NEIGH).astype(jnp.int32), axis=1).reshape(ATOMS, NEIGH)
    coords = positions.astype(jnp.float32).T
    slot_index = jnp.arange(NEIGH, dtype=jnp.int32)[None, :]

    def one_frame(rotation):

        def one_block(block_in):
            block_idx, block_count, block_centre = block_in
            live_mask = (slot_index < block_count[:, None]).astype(jnp.float32)
            return edge_messages(features[block_idx], coords[block_idx], block_centre, live_mask, rotation, w_edge, b_edge)
        message = lax.map(one_block, (edge_global.reshape(-1, 16, NEIGH), counts.reshape(-1, 16), coords.reshape(-1, 16, 3)))
        message = message.reshape(ATOMS, W).astype(jnp.bfloat16)
        hidden = jax.nn.silu(jnp.dot(message, w_message, preferred_element_type=jnp.float32)).astype(jnp.bfloat16)
        updated = (features.astype(jnp.float32) + jnp.dot(hidden, w_update, preferred_element_type=jnp.float32)).astype(jnp.bfloat16)
        readout = jax.nn.silu(jnp.dot(updated, w_readout, preferred_element_type=jnp.float32)).astype(jnp.bfloat16)
        heads = jnp.dot(readout, w_heads, preferred_element_type=jnp.float32)
        force_can = jnp.einsum('na,ac->cn', heads[:, :3], rotation, precision=lax.Precision.HIGHEST)
        return jnp.concatenate([force_can, heads[:, 3][None, :]], axis=0)
    frame_terms = lax.map(one_frame, frames)
    return lax.optimization_barrier(jnp.sum(frame_terms, axis=0)) / N_FRAME
```

```python
import jax
import jax.numpy as jnp
from jax import lax
from jax.experimental import pallas as pl
from jax.experimental.pallas import tpu as pltpu
from jax.sharding import PartitionSpec as P

BF = jnp.bfloat16
F32 = jnp.float32
I32 = jnp.int32
message_scale = 0.0884
radial_step = 1.25

ATOMS = 128
HALF = 64
CAP = 64
TABLE = CAP + ATOMS
WIDTH = 512
SLOTS = 128
FEATS = 16
GROUP = 8
GROUPS = HALF // GROUP
EXTRA = 128
PAY = WIDTH + EXTRA
RADIAL = 6
WINDOWS = ((0, 128), (16, 160), (32, 176), (48, 192))


def iota(shape, dim):
    return lax.broadcasted_iota(I32, shape, dim)


def dot(a, b):
    return jnp.dot(a, b, preferred_element_type=F32)


def dot_t(a, b):
    return lax.dot_general(a, b, (((1,), (1,)), ((), ())), preferred_element_type=F32)


def mask(cond):
    return jnp.where(cond, 1.0, 0.0).astype(F32)


def pick(cond):
    return mask(cond).astype(BF)


def pack_kernel(feat_ref, pos_ref, rows_ref, frame_ref, out_ref):
    odd = lax.axis_index("frame") % 2
    wanted = jnp.where(odd == 1, rows_ref[0, 1:2, :], rows_ref[0, 0:1, :])
    row = iota((CAP, CAP), 0)
    source = jnp.where(odd == 1, row, CAP - 1 - row)
    column = jnp.sum(
        jnp.where(iota((CAP, CAP), 1) == source, wanted, 0).astype(F32), axis=1, keepdims=True
    ).astype(I32)
    chosen = pick(iota((CAP, ATOMS), 1) == column)
    out_ref[:, :WIDTH] = dot(chosen, feat_ref[...]).astype(BF)
    lane = iota((CAP, EXTRA), 1)
    rest = jnp.zeros((CAP, EXTRA), F32)
    for c in range(3):
        line = chosen.astype(F32) * pos_ref[c : c + 1, :].astype(F32)
        rest = jnp.where(lane == c, jnp.sum(line, axis=1, keepdims=True), rest)
    turn = jnp.zeros((CAP, EXTRA), F32)
    for a in range(3):
        for c in range(3):
            k = 8 + 3 * a + c
            turn = jnp.where((lane == k) | (lane == k + 16) | (lane == k + 32), frame_ref[a, :, c : c + 1], turn)
    high = turn.astype(BF).astype(F32)
    mid = (turn - high).astype(BF).astype(F32)
    low = (turn - high - mid).astype(BF).astype(F32)
    turn = jnp.where(lane < 24, high, jnp.where(lane < 40, mid, low))
    out_ref[:, WIDTH:] = (rest + turn).astype(BF)


def main_kernel(
    pay_ref,
    feat_ref,
    pos_ref,
    nbr_ref,
    cnt_ref,
    frame_ref,
    we_ref,
    be_ref,
    wm_ref,
    wu_ref,
    wr_ref,
    wh_ref,
    out_ref,
    table,
    edges,
    rhs,
    times,
    message,
):
    odd = lax.axis_index("frame") % 2

    def local(n):
        return jnp.where(odd == 1, ATOMS - 1 - n, n)

    own = pick(iota((ATOMS, ATOMS), 1) == local(iota((ATOMS, ATOMS), 0)))
    table[:CAP, :] = pay_ref[:, :WIDTH]
    table[CAP:, :] = dot(own, feat_ref[...]).astype(BF)

    raw = nbr_ref[...]
    order = jnp.where(raw < ATOMS, raw + CAP, jnp.where(raw < ATOMS + CAP, raw - ATOMS, raw))
    order = jnp.where(odd == 1, 2 * CAP + ATOMS - 1 - order, order)
    by_slot = order.astype(F32).T.astype(BF)
    atom = local(iota((ATOMS, ATOMS), 0))
    lane = iota((ATOMS, ATOMS), 1)
    to_low = pick(atom == lane)
    to_low = jnp.where(lane < HALF, to_low, jnp.zeros_like(to_low))
    to_high = pick(atom + HALF == lane)
    folded = dot(by_slot[: SLOTS // 2], to_low) + dot(by_slot[SLOTS // 2 :], to_high)
    cnt = jnp.broadcast_to(cnt_ref[...].astype(F32), (8, ATOMS)).astype(BF)
    live = (dot(cnt, to_low) + dot(cnt, to_high))[0:1, :]
    slot = iota((SLOTS // 2, ATOMS), 0) + jnp.where(iota((SLOTS // 2, ATOMS), 1) < HALF, 0, SLOTS // 2)
    folded = jnp.where(slot.astype(F32) < live, folded, -1.0).astype(BF)
    place = iota((TABLE, ATOMS), 0).astype(F32).astype(BF)
    total = jnp.zeros((TABLE, ATOMS), BF)
    one = jnp.ones((TABLE, ATOMS), BF)
    for k in range(SLOTS // 2):
        total = jnp.where(place == folded[k : k + 1, :], total + one, total)
    for a in range(GROUP):
        spread = pick(iota((ATOMS, ATOMS), 0) % HALF == iota((ATOMS, ATOMS), 1) * GROUP + a)
        times[a, :, :] = dot(total, spread)

    lane8 = iota((8, ATOMS), 1)
    atom8 = local(lane8)
    in_group = mask(atom8 // GROUP == iota((8, ATOMS), 0))
    spread = pick(local(iota((ATOMS, ATOMS), 0)) % GROUP == lane // FEATS)
    centre = []
    reach = []
    ones = jnp.ones((ATOMS, ATOMS), BF)
    extra = pay_ref[:, WIDTH:]
    for c in range(3):
        line = pos_ref[c : c + 1, :].astype(F32)
        centre.append(dot((in_group * line).astype(BF), spread))
        mine = dot((own.astype(F32) * line).astype(BF), ones)
        ghost = dot(extra, pick(iota((EXTRA, EXTRA), 0) == c))
        reach.append(jnp.concatenate([ghost, mine], axis=0))
    kind = iota((1, ATOMS), 1) % FEATS
    shift = kind.astype(F32) * radial_step
    for g in range(GROUPS):
        lo, hi = WINDOWS[g // 2]
        rel = [reach[c][lo:hi] - centre[c][g : g + 1, :] for c in range(3)]
        dist = jnp.sqrt(rel[0] * rel[0] + rel[1] * rel[1] + rel[2] * rel[2] + 0.25) - shift
        value = jnp.exp(-(dist * dist))
        axis = jnp.where(kind % 3 == 0, rel[0], jnp.where(kind % 3 == 1, rel[1], rel[2]))
        axis_high = axis.astype(BF).astype(F32)
        axis = jnp.where((kind >= 9) & (kind < 12), axis - axis_high, axis_high)
        value = jnp.where(kind < RADIAL, value, jnp.where(kind < 15, axis, 1.0))
        edges[g, lo:hi, :] = value.astype(BF)

    turns = []
    for a in range(3):
        turns.append([(frame_ref[a, :, c : c + 1]) for c in range(3)])
    head = extra[0:1, :].astype(F32)
    other = []
    for a in range(3):
        other.append([])
        for c in range(3):
            k = 8 + 3 * a + c
            other[a].append(head[:, k : k + 1] + head[:, k + 16 : k + 17] + head[:, k + 32 : k + 33])
    block = iota((ATOMS, WIDTH), 0) // FEATS
    for f, rot in enumerate((turns, other)):
        vec = [
            0.5 * (rot[0][c] * we_ref[6:7, :] + rot[1][c] * we_ref[7:8, :] + rot[2][c] * we_ref[8:9, :])
            for c in range(3)
        ]
        vec = jnp.concatenate(vec, axis=0)
        vec_high = vec.astype(BF).astype(F32)
        rows = jnp.concatenate(
            [0.5 * we_ref[0:RADIAL, :], vec_high, vec_high, vec - vec_high, 0.5 * be_ref[...]], axis=0
        )
        rows = jnp.concatenate([rows] * GROUP, axis=0).astype(BF)
        for a in range(GROUP):
            rhs[a, :, f * WIDTH : (f + 1) * WIDTH] = jnp.where(block == a, rows, jnp.zeros_like(rows))

    tile = 256

    def step(a, carry):
        share = times[a].astype(BF)
        for w in range(WIDTH // tile):
            span = slice(w * tile, (w + 1) * tile)
            for g in range(GROUPS):
                lo, hi = WINDOWS[g // 2]
                weighted = table[lo:hi, span] * share[lo:hi, g : g + 1]
                for f in range(2):
                    pre = dot(edges[g, lo:hi, :], rhs[a, :, f * WIDTH + w * tile : f * WIDTH + (w + 1) * tile])
                    half = pre.astype(BF)
                    gate = half * jnp.tanh(half) + half
                    prod = gate * weighted
                    parts = [prod[r : r + 16] for r in range(0, hi - lo, 16)]
                    quads = [
                        (parts[q] + parts[q + 1]) + (parts[q + 2] + parts[q + 3])
                        for q in range(0, len(parts) - 3, 4)
                    ] + parts[len(parts) // 4 * 4 :]
                    total = quads[0].astype(F32)
                    for q in quads[1:]:
                        total = total + q.astype(F32)
                    message[a, f * GROUPS + g : f * GROUPS + g + 1, span] = jnp.sum(
                        total, axis=0, keepdims=True
                    )
        return carry

    lax.fori_loop(0, GROUP, step, 0)

    msg = (message[...].reshape(ATOMS, WIDTH) * message_scale).astype(BF)
    row = iota((ATOMS, ATOMS), 0)
    row_atom = (row % GROUPS) * GROUP + row // 16
    mine = dot(pick(lane == local(row_atom)), feat_ref[...])

    def silu(x):
        h = 0.5 * x
        return h * jnp.tanh(h) + h

    hidden = silu(dot(msg, wm_ref[...])).astype(BF)
    updated = (mine + dot(hidden, wu_ref[...])).astype(BF)
    readout = silu(dot(updated, wr_ref[...])).astype(BF)
    lane_atom = (lane % GROUPS) * GROUP + lane // 16
    total = jnp.zeros((4, ATOMS), F32)
    for f, rot in enumerate((turns, other)):
        back = pick((local(row) == lane_atom) & ((lane // GROUPS) % 2 == f))
        placed = dot(back, readout).astype(BF)
        heads = dot_t(wh_ref[...], placed)
        force = [
            rot[0][c] * heads[0:1] + rot[1][c] * heads[1:2] + rot[2][c] * heads[2:3] for c in range(3)
        ]
        total = total + jnp.concatenate(force + [heads[3:4]], axis=0)
    out_ref[...] = total


def local_step(
    features,
    positions,
    neighbours,
    counts,
    send_rows,
    frames,
    w_edge,
    b_edge,
    w_message,
    w_update,
    w_readout,
    w_heads,
):
    dom_count = lax.axis_size("dom")
    frame_count = lax.axis_size("frame")
    frame = jnp.transpose(frames, (1, 0, 2))
    payload = pl.pallas_call(
        pack_kernel,
        out_shape=jax.ShapeDtypeStruct((CAP, PAY), BF),
    )(features, positions, send_rows, frame)
    pairs = []
    for d in range(dom_count):
        for f in range(frame_count):
            to = (d + 1) % dom_count if f % 2 else (d - 1) % dom_count
            pairs.append((d * frame_count + f, to * frame_count + (f ^ 1)))
    ghosts = lax.ppermute(payload, ("dom", "frame"), pairs)
    part = pl.pallas_call(
        main_kernel,
        out_shape=jax.ShapeDtypeStruct((4, ATOMS), F32),
        scratch_shapes=[
            pltpu.VMEM((TABLE, WIDTH), BF),
            pltpu.VMEM((GROUPS, TABLE, ATOMS), BF),
            pltpu.VMEM((GROUP, ATOMS, 2 * WIDTH), BF),
            pltpu.VMEM((GROUP, TABLE, ATOMS), F32),
            pltpu.VMEM((GROUP, 2 * GROUPS, WIDTH), F32),
        ],
        compiler_params=pltpu.CompilerParams(vmem_limit_bytes=32 << 20),
    )(
        ghosts,
        features,
        positions,
        neighbours,
        counts.reshape(1, ATOMS),
        frame,
        w_edge,
        b_edge.reshape(1, WIDTH),
        w_message,
        w_update,
        w_readout,
        w_heads.T,
    )
    copies = jnp.broadcast_to(part, (frame_count, *part.shape))
    everything = lax.all_to_all(copies, "frame", split_axis=0, concat_axis=0, tiled=True)
    return jnp.sum(everything, axis=0) / frame_count


def solution(mesh):
    placed = (
        P("dom", None),
        P(None, "dom"),
        P("dom", None),
        P("dom"),
        P("dom", None, None),
        P("frame", None, None),
        P(),
        P(),
        P(),
        P(),
        P(),
        P(),
    )
    return jax.shard_map(
        local_step, mesh=mesh, in_specs=placed, out_specs=P(None, "dom"), check_vma=False
    )
```

```python
import jax
import jax.numpy as jnp
from jax import lax
from jax.experimental import pallas as pl
from jax.experimental.pallas import tpu as pltpu
from jax.sharding import PartitionSpec as P

BF = jnp.bfloat16
F32 = jnp.float32
I32 = jnp.int32
message_scale = 0.0884
radial_step = 1.25

ATOMS = 128
HALF = 64
CAP = 64
TABLE = CAP + ATOMS
WIDTH = 512
SLOTS = 128
FEATS = 16
GROUP = 8
GROUPS = HALF // GROUP
EXTRA = 128
PAY = WIDTH + EXTRA
RADIAL = 6
GHOST_ROWS = ((0, 64), (16, 64), (32, 64), (48, 64))
OWN_ROWS = ((0, 64), (0, 96), (0, 112), (0, 128))
TILE = 256


def iota(shape, dim):
    return lax.broadcasted_iota(I32, shape, dim)


def dot(a, b):
    return jnp.dot(a, b, preferred_element_type=F32)


def dot_t(a, b):
    return lax.dot_general(a, b, (((1,), (1,)), ((), ())), preferred_element_type=F32)


def mask(cond):
    return jnp.where(cond, 1.0, 0.0).astype(F32)


def pick(cond):
    return mask(cond).astype(BF)


def parity():
    return lax.axis_index("frame") % 2


def local(n):
    return jnp.where(parity() == 1, ATOMS - 1 - n, n)


def entries(ref):
    return [[ref[a, :, c : c + 1] for c in range(3)] for a in range(3)]


def vectors(rot, we_ref, c):
    return 0.5 * (rot[0][c] * we_ref[6:7, :] + rot[1][c] * we_ref[7:8, :] + rot[2][c] * we_ref[8:9, :])


def split(x):
    high = x.astype(BF).astype(F32)
    return high, x - high


def centres(pos_ref):
    atom = local(iota((8, ATOMS), 1))
    in_group = mask(atom // GROUP == iota((8, ATOMS), 0))
    spread = pick(local(iota((ATOMS, ATOMS), 0)) % GROUP == iota((ATOMS, ATOMS), 1) // FEATS)
    return [dot((in_group * pos_ref[c : c + 1, :].astype(F32)).astype(BF), spread) for c in range(3)]


def placed_rows(chosen, pos_ref):
    ones = jnp.ones((ATOMS, ATOMS), BF)
    return [dot((chosen * pos_ref[c : c + 1, :].astype(F32)).astype(BF), ones) for c in range(3)]


def fill_edges(edges, reach, centre, bounds):
    kind = iota((1, ATOMS), 1) % FEATS
    shift = kind.astype(F32) * radial_step
    at = 0
    for g in range(GROUPS):
        lo, hi = bounds[g // 2]
        rel = [reach[c][lo:hi] - centre[c][g : g + 1, :] for c in range(3)]
        dist = jnp.sqrt(rel[0] * rel[0] + rel[1] * rel[1] + rel[2] * rel[2] + 0.25) - shift
        value = jnp.exp(-(dist * dist))
        axis = jnp.where(kind % 3 == 0, rel[0], jnp.where(kind % 3 == 1, rel[1], rel[2]))
        high, low = split(axis)
        axis = jnp.where((kind >= 9) & (kind < 12), low, high)
        value = jnp.where(kind < RADIAL, value, jnp.where(kind < 15, axis, 1.0))
        edges[at : at + hi - lo, :] = value.astype(BF)
        at += hi - lo


def fill_filter(rhs, rot, we_ref, be_ref):
    vec = jnp.concatenate([vectors(rot, we_ref, c) for c in range(3)], axis=0)
    high, low = split(vec)
    rows = jnp.concatenate([0.5 * we_ref[0:RADIAL, :], high, high, low, 0.5 * be_ref[...]], axis=0)
    rows = jnp.concatenate([rows] * GROUP, axis=0).astype(BF)
    block = iota((ATOMS, WIDTH), 0) // FEATS
    for a in range(GROUP):
        rhs[a, :, :] = jnp.where(block == a, rows, jnp.zeros_like(rows))


def from_middle(reach):
    lane = iota((1, ATOMS), 1)
    axis = jnp.where(lane % 3 == 0, reach[0], jnp.where(lane % 3 == 1, reach[1], reach[2])) - 2.0
    high, low = split(axis)
    axis = jnp.where((lane >= 3) & (lane < 6), low, high)
    return jnp.where(lane < 9, axis, 0.0).astype(BF)


def change_filter(rot, other, we_ref):
    vec = jnp.concatenate([vectors(other, we_ref, c) - vectors(rot, we_ref, c) for c in range(3)], axis=0)
    high, low = split(vec)
    return jnp.concatenate([high, high, low, jnp.zeros((ATOMS - 9, WIDTH), F32)], axis=0).astype(BF)


def fill_change(change, middle, pos_ref, reach, rot, other, we_ref):
    weights = change_filter(rot, other, we_ref)
    change[...] = dot(from_middle(reach), weights).astype(BF)
    row = iota((HALF, ATOMS), 0)
    chosen = mask(local(iota((HALF, ATOMS), 1)) == (row % GROUPS) * GROUP + row // GROUPS)
    middle[...] = dot(from_middle(placed_rows(chosen, pos_ref)), weights).astype(BF).astype(F32)


def fill_times(times, total):
    for a in range(GROUP):
        spread = pick(iota((ATOMS, ATOMS), 0) % HALF == iota((ATOMS, ATOMS), 1) * GROUP + a)
        times[a, :, :] = dot(total, spread)


def sum_rows(prod, rows):
    parts = [prod[r : r + 16] for r in range(0, rows, 16)]
    while len(parts) > SUMS:
        parts = [
            parts[q] + parts[q + 1] if q + 1 < len(parts) else parts[q] for q in range(0, len(parts), 2)
        ]
    total = parts[0].astype(F32)
    for part in parts[1:]:
        total = total + part.astype(F32)
    return total[:8] + total[8:]


SUMS = 2


def pair_loop(bounds, merge, table, edges, rhs, times, change, middle, partial):
    offsets = [0]
    for g in range(GROUPS):
        lo, hi = bounds[g // 2]
        offsets.append(offsets[-1] + hi - lo)

    def step(a, carry):
        share = times[a].astype(BF)
        centre = middle[pl.ds(pl.multiple_of(a * GROUPS, GROUPS), GROUPS), :]
        for w in range(WIDTH // TILE):
            span = slice(w * TILE, (w + 1) * TILE)
            for first in range(0, GROUPS, merge):
                pre = dot(edges[offsets[first] : offsets[first + merge], :], rhs[a, :, span]).astype(BF)
                for g in range(first, first + merge):
                    lo, hi = bounds[g // 2]
                    weighted = table[lo:hi, span] * share[lo:hi, g : g + 1]
                    half = pre[offsets[g] - offsets[first] : offsets[g + 1] - offsets[first]]
                    for f in range(2):
                        if f == 1:
                            half = half + (change[lo:hi, span] - centre[g : g + 1, span].astype(BF))
                        gate = half * jnp.tanh(half) + half
                        at = pl.multiple_of(a * (16 * 8) + (f * GROUPS + g) * 8, 8)
                        done = sum_rows(gate * weighted, hi - lo)
                        for t in range(TILE // 128):
                            partial[w * (TILE // 128) + t, pl.ds(at, 8), :] = done[:, t * 128 : (t + 1) * 128]
        return carry

    lax.fori_loop(0, GROUP, step, 0)
    tiles = []
    for t in range(WIDTH // 128):
        total = partial[t, pl.ds(0, ATOMS, stride=8), :]
        for r in range(1, 8):
            total = total + partial[t, pl.ds(r, ATOMS, stride=8), :]
        tiles.append(total)
    return jnp.concatenate(tiles, axis=1)


def pack_kernel(feat_ref, pos_ref, rows_ref, out_ref):
    wanted = jnp.where(parity() == 1, rows_ref[0, 1:2, :], rows_ref[0, 0:1, :])
    row = iota((CAP, CAP), 0)
    source = jnp.where(parity() == 1, row, CAP - 1 - row)
    column = jnp.sum(
        jnp.where(iota((CAP, CAP), 1) == source, wanted, 0).astype(F32), axis=1, keepdims=True
    ).astype(I32)
    chosen = pick(iota((CAP, ATOMS), 1) == column)
    out_ref[:, :WIDTH] = dot(chosen, feat_ref[...]).astype(BF)
    lane = iota((CAP, EXTRA), 1)
    rest = jnp.zeros((CAP, EXTRA), F32)
    for c in range(3):
        line = chosen.astype(F32) * pos_ref[c : c + 1, :].astype(F32)
        rest = jnp.where(lane == c, jnp.sum(line, axis=1, keepdims=True), rest)
    out_ref[:, WIDTH:] = rest.astype(BF)


def own_kernel(
    feat_ref,
    pos_ref,
    nbr_ref,
    cnt_ref,
    frame_ref,
    other_ref,
    we_ref,
    be_ref,
    sum_ref,
    ghost_ref,
    table,
    edges,
    rhs,
    times,
    change,
    middle,
    partial,
):
    own = pick(iota((ATOMS, ATOMS), 1) == local(iota((ATOMS, ATOMS), 0)))
    table[...] = dot(own, feat_ref[...]).astype(BF)

    raw = nbr_ref[...]
    order = jnp.where(raw < ATOMS, raw + CAP, jnp.where(raw < ATOMS + CAP, raw - ATOMS, raw))
    order = jnp.where(parity() == 1, 2 * CAP + ATOMS - 1 - order, order)
    by_slot = order.astype(F32).T.astype(BF)
    atom = local(iota((ATOMS, ATOMS), 0))
    lane = iota((ATOMS, ATOMS), 1)
    to_low = pick((atom == lane) & (lane < HALF))
    to_high = pick(atom + HALF == lane)
    folded = dot(by_slot[: SLOTS // 2], to_low) + dot(by_slot[SLOTS // 2 :], to_high)
    cnt = jnp.broadcast_to(cnt_ref[...].astype(F32), (8, ATOMS)).astype(BF)
    live = (dot(cnt, to_low) + dot(cnt, to_high))[0:1, :]
    slot = iota((SLOTS // 2, ATOMS), 0) + jnp.where(iota((SLOTS // 2, ATOMS), 1) < HALF, 0, SLOTS // 2)
    folded = jnp.where(slot.astype(F32) < live, folded, -1.0).astype(BF)
    place = iota((TABLE, ATOMS), 0).astype(F32).astype(BF)
    total = jnp.zeros((TABLE, ATOMS), BF)
    one = jnp.ones((TABLE, ATOMS), BF)
    for k in range(SLOTS // 2):
        total = jnp.where(place == folded[k : k + 1, :], total + one, total)
    ghost_ref[...] = total[:CAP]
    fill_times(times, total[CAP:])

    rot, other = entries(frame_ref), entries(other_ref)
    reach = placed_rows(own.astype(F32), pos_ref)
    fill_edges(edges, reach, centres(pos_ref), OWN_ROWS)
    fill_filter(rhs, rot, we_ref, be_ref)
    fill_change(change, middle, pos_ref, reach, rot, other, we_ref)
    sum_ref[...] = pair_loop(OWN_ROWS, 1, table, edges, rhs, times, change, middle, partial)


def last_kernel(
    pay_ref,
    sum_ref,
    ghost_ref,
    feat_ref,
    pos_ref,
    frame_ref,
    other_ref,
    we_ref,
    be_ref,
    wm_ref,
    wu_ref,
    wr_ref,
    wh_ref,
    out_ref,
    edges,
    rhs,
    times,
    change,
    middle,
    partial,
):
    rot, other = entries(frame_ref), entries(other_ref)
    extra = pay_ref[:, WIDTH:]
    reach = [dot(extra, pick(iota((EXTRA, EXTRA), 0) == c)) for c in range(3)]
    fill_times(times, ghost_ref[...])
    fill_edges(edges, reach, centres(pos_ref), GHOST_ROWS)
    fill_filter(rhs, rot, we_ref, be_ref)
    fill_change(change, middle, pos_ref, reach, rot, other, we_ref)
    total = pair_loop(GHOST_ROWS, GROUPS, pay_ref, edges, rhs, times, change, middle, partial)

    msg = ((total + sum_ref[...]) * message_scale).astype(BF)
    row = iota((ATOMS, ATOMS), 0)
    lane = iota((ATOMS, ATOMS), 1)
    row_atom = (row % GROUPS) * GROUP + row // 16
    mine = dot(pick(lane == local(row_atom)), feat_ref[...])

    def silu(x):
        h = 0.5 * x
        return h * jnp.tanh(h) + h

    hidden = silu(dot(msg, wm_ref[...])).astype(BF)
    updated = (mine + dot(hidden, wu_ref[...])).astype(BF)
    readout = silu(dot(updated, wr_ref[...])).astype(BF)
    lane_atom = (lane % GROUPS) * GROUP + lane // 16
    out = jnp.zeros((4, ATOMS), F32)
    for f, turn in enumerate((rot, other)):
        back = pick((local(row) == lane_atom) & ((lane // GROUPS) % 2 == f))
        heads = dot_t(wh_ref[...], dot(back, readout).astype(BF))
        force = [
            turn[0][c] * heads[0:1] + turn[1][c] * heads[1:2] + turn[2][c] * heads[2:3] for c in range(3)
        ]
        out = out + jnp.concatenate(force + [heads[3:4]], axis=0)
    out_ref[...] = out


def scratch(rows, edge_rows):
    return [
        pltpu.VMEM((edge_rows, ATOMS), BF),
        pltpu.VMEM((GROUP, ATOMS, WIDTH), BF),
        pltpu.VMEM((GROUP, rows, ATOMS), F32),
        pltpu.VMEM((rows, WIDTH), BF),
        pltpu.VMEM((HALF, WIDTH), F32),
        pltpu.VMEM((WIDTH // 128, ATOMS * 8, 128), F32),
    ]


def local_step(
    features,
    positions,
    neighbours,
    counts,
    send_rows,
    frames,
    w_edge,
    b_edge,
    w_message,
    w_update,
    w_readout,
    w_heads,
):
    dom_count = lax.axis_size("dom")
    frame_count = lax.axis_size("frame")
    frame = jnp.transpose(frames, (1, 0, 2))
    other = lax.ppermute(frame, "frame", [(f, f ^ 1) for f in range(frame_count)])
    payload = pl.pallas_call(
        pack_kernel,
        out_shape=jax.ShapeDtypeStruct((CAP, PAY), BF),
    )(features, positions, send_rows)
    pairs = []
    for d in range(dom_count):
        for f in range(frame_count):
            to = (d + 1) % dom_count if f % 2 else (d - 1) % dom_count
            pairs.append((d * frame_count + f, to * frame_count + (f ^ 1)))
    ghosts = lax.ppermute(payload, ("dom", "frame"), pairs)
    bias = b_edge.reshape(1, WIDTH)
    own_rows = 2 * sum(hi - lo for lo, hi in OWN_ROWS)
    ghost_rows = 2 * sum(hi - lo for lo, hi in GHOST_ROWS)
    own_sum, ghost_times = pl.pallas_call(
        own_kernel,
        out_shape=[
            jax.ShapeDtypeStruct((ATOMS, WIDTH), F32),
            jax.ShapeDtypeStruct((CAP, ATOMS), BF),
        ],
        scratch_shapes=[pltpu.VMEM((ATOMS, WIDTH), BF)] + scratch(ATOMS, own_rows),
        compiler_params=pltpu.CompilerParams(vmem_limit_bytes=24 << 20),
        cost_estimate=pl.CostEstimate(flops=2_000_000_000, bytes_accessed=1_000_000, transcendentals=7_000_000),
    )(features, positions, neighbours, counts.reshape(1, ATOMS), frame, other, w_edge, bias)
    part = pl.pallas_call(
        last_kernel,
        out_shape=jax.ShapeDtypeStruct((4, ATOMS), F32),
        scratch_shapes=scratch(CAP, ghost_rows),
        compiler_params=pltpu.CompilerParams(vmem_limit_bytes=24 << 20),
    )(
        ghosts,
        own_sum,
        ghost_times,
        features,
        positions,
        frame,
        other,
        w_edge,
        bias,
        w_message,
        w_update,
        w_readout,
        w_heads.T,
    )
    copies = jnp.broadcast_to(part, (frame_count, *part.shape))
    everything = lax.all_to_all(copies, "frame", split_axis=0, concat_axis=0, tiled=True)
    return jnp.sum(everything, axis=0) / frame_count


def solution(mesh):
    placed = (
        P("dom", None),
        P(None, "dom"),
        P("dom", None),
        P("dom"),
        P("dom", None, None),
        P("frame", None, None),
        P(),
        P(),
        P(),
        P(),
        P(),
        P(),
    )
    return jax.shard_map(
        local_step, mesh=mesh, in_specs=placed, out_specs=P(None, "dom"), check_vma=False
    )
```

```python
import jax
import jax.numpy as jnp
from jax import lax
from jax.experimental import pallas as pl
from jax.experimental.pallas import tpu as pltpu
from jax.sharding import PartitionSpec as P

BF = jnp.bfloat16
F32 = jnp.float32
I32 = jnp.int32
message_scale = 0.0884
radial_step = 1.25

ATOMS = 128
HALF = 64
CAP = 64
TABLE = CAP + ATOMS
WIDTH = 512
SLOTS = 128
FEATS = 16
GROUP = 8
GROUPS = HALF // GROUP
EXTRA = 128
PAY = WIDTH + EXTRA
RADIAL = 6
GHOST_ROWS = ((0, 64), (16, 64), (32, 64), (48, 64))
OWN_ROWS = ((0, 64), (0, 96), (0, 112), (0, 128))
TILE = 256


def iota(shape, dim):
    return lax.broadcasted_iota(I32, shape, dim)


def dot(a, b):
    return jnp.dot(a, b, preferred_element_type=F32)


def dot_t(a, b):
    return lax.dot_general(a, b, (((1,), (1,)), ((), ())), preferred_element_type=F32)


def mask(cond):
    return jnp.where(cond, 1.0, 0.0).astype(F32)


def pick(cond):
    return mask(cond).astype(BF)


def parity():
    return lax.axis_index("frame") % 2


def local(n):
    return jnp.where(parity() == 1, ATOMS - 1 - n, n)


def entries(ref):
    return [[ref[a, :, c : c + 1] for c in range(3)] for a in range(3)]


def vectors(rot, we_ref, c):
    return 0.5 * (rot[0][c] * we_ref[6:7, :] + rot[1][c] * we_ref[7:8, :] + rot[2][c] * we_ref[8:9, :])


def split(x):
    high = x.astype(BF).astype(F32)
    return high, x - high


def centres(pos_ref):
    atom = local(iota((8, ATOMS), 1))
    in_group = mask(atom // GROUP == iota((8, ATOMS), 0))
    spread = pick(local(iota((ATOMS, ATOMS), 0)) % GROUP == iota((ATOMS, ATOMS), 1) // FEATS)
    return [dot((in_group * pos_ref[c : c + 1, :].astype(F32)).astype(BF), spread) for c in range(3)]


def placed_rows(chosen, pos_ref):
    ones = jnp.ones((ATOMS, ATOMS), BF)
    return [dot((chosen * pos_ref[c : c + 1, :].astype(F32)).astype(BF), ones) for c in range(3)]


def fill_edges(edges, reach, centre, bounds):
    kind = iota((1, ATOMS), 1) % FEATS
    shift = kind.astype(F32) * radial_step
    at = 0
    for g in range(GROUPS):
        lo, hi = bounds[g // 2]
        rel = [reach[c][lo:hi] - centre[c][g : g + 1, :] for c in range(3)]
        dist = jnp.sqrt(rel[0] * rel[0] + rel[1] * rel[1] + rel[2] * rel[2] + 0.25) - shift
        value = jnp.exp(-(dist * dist))
        axis = jnp.where(kind % 3 == 0, rel[0], jnp.where(kind % 3 == 1, rel[1], rel[2]))
        high, low = split(axis)
        axis = jnp.where((kind >= 9) & (kind < 12), low, high)
        value = jnp.where(kind < RADIAL, value, jnp.where(kind < 15, axis, 1.0))
        edges[at : at + hi - lo, :] = value.astype(BF)
        at += hi - lo


def fill_filter(rhs, rot, we_ref, be_ref):
    vec = jnp.concatenate([vectors(rot, we_ref, c) for c in range(3)], axis=0)
    high, low = split(vec)
    rows = jnp.concatenate([0.5 * we_ref[0:RADIAL, :], high, high, low, 0.5 * be_ref[...]], axis=0)
    rows = jnp.concatenate([rows] * GROUP, axis=0).astype(BF)
    block = iota((ATOMS, WIDTH), 0) // FEATS
    for a in range(GROUP):
        rhs[a, :, :] = jnp.where(block == a, rows, jnp.zeros_like(rows))


def fill_times(times, total):
    for a in range(GROUP):
        spread = pick(iota((ATOMS, ATOMS), 0) % HALF == iota((ATOMS, ATOMS), 1) * GROUP + a)
        times[a, :, :] = dot(total, spread)


def sum_rows(prod, rows):
    parts = [prod[r : r + 16] for r in range(0, rows, 16)]
    while len(parts) > SUMS:
        parts = [
            parts[q] + parts[q + 1] if q + 1 < len(parts) else parts[q] for q in range(0, len(parts), 2)
        ]
    total = parts[0].astype(F32)
    for part in parts[1:]:
        total = total + part.astype(F32)
    return total[:8] + total[8:]


SUMS = 2


def offsets_of(bounds):
    offsets = [0]
    for g in range(GROUPS):
        lo, hi = bounds[g // 2]
        offsets.append(offsets[-1] + hi - lo)
    return offsets


OWN_AT = offsets_of(OWN_ROWS)
GHOST_AT = offsets_of(GHOST_ROWS)


def gated(pre):
    half = pre.astype(BF)
    return half * jnp.tanh(half) + half


def cut(rows):
    return [rows[r : r + 16] for r in range(0, rows.shape[0], 16)]


def total_of(parts):
    while len(parts) > SUMS:
        parts = [
            parts[q] + parts[q + 1] if q + 1 < len(parts) else parts[q] for q in range(0, len(parts), 2)
        ]
    total = parts[0].astype(F32)
    for part in parts[1:]:
        total = total + part.astype(F32)
    return total[:8] + total[8:]


def keep(partial, a, k, count, w, done):
    at = pl.multiple_of((a * count + k) * 8, 8)
    for t in range(TILE // 128):
        partial[w * (TILE // 128) + t, pl.ds(at, 8), :] = done[:, t * 128 : (t + 1) * 128]


def collect(partial, rows):
    tiles = []
    for t in range(WIDTH // 128):
        total = partial[t, pl.ds(0, rows, stride=8), :]
        for r in range(1, 8):
            total = total + partial[t, pl.ds(r, rows, stride=8), :]
        tiles.append(total)
    return jnp.concatenate(tiles, axis=1)


def pack_kernel(feat_ref, pos_ref, rows_ref, frame_ref, out_ref):
    wanted = jnp.where(parity() == 1, rows_ref[0, 1:2, :], rows_ref[0, 0:1, :])
    row = iota((CAP, CAP), 0)
    source = jnp.where(parity() == 1, row, CAP - 1 - row)
    column = jnp.sum(
        jnp.where(iota((CAP, CAP), 1) == source, wanted, 0).astype(F32), axis=1, keepdims=True
    ).astype(I32)
    chosen = pick(iota((CAP, ATOMS), 1) == column)
    out_ref[:, :WIDTH] = dot(chosen, feat_ref[...]).astype(BF)
    lane = iota((CAP, EXTRA), 1)
    rest = jnp.zeros((CAP, EXTRA), F32)
    for c in range(3):
        line = chosen.astype(F32) * pos_ref[c : c + 1, :].astype(F32)
        rest = jnp.where(lane == c, jnp.sum(line, axis=1, keepdims=True), rest)
    turn = jnp.zeros((CAP, EXTRA), F32)
    for a in range(3):
        for c in range(3):
            k = 8 + 3 * a + c
            here = (lane == k) | (lane == k + 16) | (lane == k + 32)
            turn = jnp.where(here, frame_ref[a, :, c : c + 1], turn)
    high, rest_of = split(turn)
    mid, low = split(rest_of)
    turn = jnp.where(lane < 24, high, jnp.where(lane < 40, mid, low))
    out_ref[:, WIDTH:] = (rest + turn).astype(BF)


def own_kernel(
    feat_ref,
    pos_ref,
    nbr_ref,
    cnt_ref,
    frame_ref,
    we_ref,
    be_ref,
    sum_ref,
    total_ref,
    table,
    edges,
    rhs,
    times,
    partial,
):
    own = pick(iota((ATOMS, ATOMS), 1) == local(iota((ATOMS, ATOMS), 0)))
    table[...] = dot(own, feat_ref[...]).astype(BF)

    raw = nbr_ref[...]
    order = jnp.where(raw < ATOMS, raw + CAP, jnp.where(raw < ATOMS + CAP, raw - ATOMS, raw))
    order = jnp.where(parity() == 1, 2 * CAP + ATOMS - 1 - order, order)
    by_slot = order.astype(F32).T.astype(BF)
    atom = local(iota((ATOMS, ATOMS), 0))
    lane = iota((ATOMS, ATOMS), 1)
    to_low = pick((atom == lane) & (lane < HALF))
    to_high = pick(atom + HALF == lane)
    folded = dot(by_slot[: SLOTS // 2], to_low) + dot(by_slot[SLOTS // 2 :], to_high)
    cnt = jnp.broadcast_to(cnt_ref[...].astype(F32), (8, ATOMS)).astype(BF)
    live = (dot(cnt, to_low) + dot(cnt, to_high))[0:1, :]
    slot = iota((SLOTS // 2, ATOMS), 0) + jnp.where(iota((SLOTS // 2, ATOMS), 1) < HALF, 0, SLOTS // 2)
    folded = jnp.where(slot.astype(F32) < live, folded, -1.0).astype(BF)
    place = iota((TABLE, ATOMS), 0).astype(F32).astype(BF)
    total = jnp.zeros((TABLE, ATOMS), BF)
    one = jnp.ones((TABLE, ATOMS), BF)
    for k in range(SLOTS // 2):
        total = jnp.where(place == folded[k : k + 1, :], total + one, total)
    total_ref[...] = total
    fill_times(times, total[CAP:])
    fill_edges(edges, placed_rows(own.astype(F32), pos_ref), centres(pos_ref), OWN_ROWS)
    fill_filter(rhs, entries(frame_ref), we_ref, be_ref)

    def step(a, carry):
        share = times[a].astype(BF)
        for w in range(WIDTH // TILE):
            span = slice(w * TILE, (w + 1) * TILE)
            for g in range(GROUPS):
                lo, hi = OWN_ROWS[g // 2]
                weighted = table[lo:hi, span] * share[lo:hi, g : g + 1]
                gate = gated(dot(edges[OWN_AT[g] : OWN_AT[g + 1], :], rhs[a, :, span]))
                keep(partial, a, g, GROUPS, w, total_of(cut(gate * weighted)))
        return carry

    lax.fori_loop(0, GROUP, step, 0)
    sum_ref[...] = collect(partial, HALF)


def last_kernel(
    pay_ref,
    sum_ref,
    total_ref,
    table,
    edges,
    feat_ref,
    pos_ref,
    frame_ref,
    we_ref,
    be_ref,
    wm_ref,
    wu_ref,
    wr_ref,
    wh_ref,
    out_ref,
    ghosts,
    rhs,
    rhs_other,
    times,
    partial,
):
    rot = entries(frame_ref)
    extra = pay_ref[:, WIDTH:]
    head = extra[0:1, :].astype(F32)
    other = []
    for a in range(3):
        other.append([])
        for c in range(3):
            k = 8 + 3 * a + c
            other[a].append(head[:, k : k + 1] + head[:, k + 16 : k + 17] + head[:, k + 32 : k + 33])
    reach = [dot(extra, pick(iota((EXTRA, EXTRA), 0) == c)) for c in range(3)]
    fill_times(times, total_ref[...])
    fill_edges(ghosts, reach, centres(pos_ref), GHOST_ROWS)
    fill_filter(rhs, rot, we_ref, be_ref)
    fill_filter(rhs_other, other, we_ref, be_ref)

    def step(a, carry):
        share = times[a].astype(BF)
        for w in range(WIDTH // TILE):
            span = slice(w * TILE, (w + 1) * TILE)
            near = gated(dot(ghosts[...], rhs[a, :, span]))
            far = gated(dot(ghosts[...], rhs_other[a, :, span]))
            for g in range(GROUPS):
                lo, hi = GHOST_ROWS[g // 2]
                weighted = pay_ref[lo:hi, span] * share[lo:hi, g : g + 1]
                rows = slice(GHOST_AT[g], GHOST_AT[g + 1])
                keep(partial, a, g, 2 * GROUPS, w, total_of(cut(near[rows] * weighted)))
                parts = cut(far[rows] * weighted)
                lo, hi = OWN_ROWS[g // 2]
                weighted = table[lo:hi, span] * share[CAP + lo : CAP + hi, g : g + 1]
                gate = gated(dot(edges[OWN_AT[g] : OWN_AT[g + 1], :], rhs_other[a, :, span]))
                parts = parts + cut(gate * weighted)
                keep(partial, a, GROUPS + g, 2 * GROUPS, w, total_of(parts))
        return carry

    lax.fori_loop(0, GROUP, step, 0)
    total = collect(partial, ATOMS)
    before = [
        piece
        for a in range(GROUP)
        for piece in (sum_ref[a * GROUPS : (a + 1) * GROUPS, :], jnp.zeros((GROUPS, WIDTH), F32))
    ]
    msg = ((total + jnp.concatenate(before, axis=0)) * message_scale).astype(BF)
    row = iota((ATOMS, ATOMS), 0)
    lane = iota((ATOMS, ATOMS), 1)
    row_atom = (row % GROUPS) * GROUP + row // 16
    mine = dot(pick(lane == local(row_atom)), feat_ref[...])

    def silu(x):
        h = 0.5 * x
        return h * jnp.tanh(h) + h

    hidden = silu(dot(msg, wm_ref[...])).astype(BF)
    updated = (mine + dot(hidden, wu_ref[...])).astype(BF)
    readout = silu(dot(updated, wr_ref[...])).astype(BF)
    lane_atom = (lane % GROUPS) * GROUP + lane // 16
    out = jnp.zeros((4, ATOMS), F32)
    for f, turn in enumerate((rot, other)):
        back = pick((local(row) == lane_atom) & ((lane // GROUPS) % 2 == f))
        heads = dot_t(wh_ref[...], dot(back, readout).astype(BF))
        force = [
            turn[0][c] * heads[0:1] + turn[1][c] * heads[1:2] + turn[2][c] * heads[2:3] for c in range(3)
        ]
        out = out + jnp.concatenate(force + [heads[3:4]], axis=0)
    out_ref[...] = out


def cost(microseconds):
    return pl.CostEstimate(flops=microseconds * 10**9, bytes_accessed=microseconds * 10**6, transcendentals=0)


def local_step(
    features,
    positions,
    neighbours,
    counts,
    send_rows,
    frames,
    w_edge,
    b_edge,
    w_message,
    w_update,
    w_readout,
    w_heads,
):
    dom_count = lax.axis_size("dom")
    frame_count = lax.axis_size("frame")
    frame = jnp.transpose(frames, (1, 0, 2))
    payload = pl.pallas_call(
        pack_kernel,
        out_shape=jax.ShapeDtypeStruct((CAP, PAY), BF),
        cost_estimate=cost(2),
    )(features, positions, send_rows, frame)
    pairs = []
    for d in range(dom_count):
        for f in range(frame_count):
            to = (d + 1) % dom_count if f % 2 else (d - 1) % dom_count
            pairs.append((d * frame_count + f, to * frame_count + (f ^ 1)))
    ghosts = lax.ppermute(payload, ("dom", "frame"), pairs)
    bias = b_edge.reshape(1, WIDTH)
    own_sum, total, table, edges = pl.pallas_call(
        own_kernel,
        out_shape=[
            jax.ShapeDtypeStruct((HALF, WIDTH), F32),
            jax.ShapeDtypeStruct((TABLE, ATOMS), BF),
            jax.ShapeDtypeStruct((ATOMS, WIDTH), BF),
            jax.ShapeDtypeStruct((OWN_AT[-1], ATOMS), BF),
        ],
        scratch_shapes=[
            pltpu.VMEM((GROUP, ATOMS, WIDTH), BF),
            pltpu.VMEM((GROUP, ATOMS, ATOMS), F32),
            pltpu.VMEM((WIDTH // 128, HALF * 8, 128), F32),
        ],
        compiler_params=pltpu.CompilerParams(vmem_limit_bytes=24 << 20),
        cost_estimate=cost(5),
    )(features, positions, neighbours, counts.reshape(1, ATOMS), frame, w_edge, bias)
    part = pl.pallas_call(
        last_kernel,
        out_shape=jax.ShapeDtypeStruct((4, ATOMS), F32),
        scratch_shapes=[
            pltpu.VMEM((GHOST_AT[-1], ATOMS), BF),
            pltpu.VMEM((GROUP, ATOMS, WIDTH), BF),
            pltpu.VMEM((GROUP, ATOMS, WIDTH), BF),
            pltpu.VMEM((GROUP, TABLE, ATOMS), F32),
            pltpu.VMEM((WIDTH // 128, ATOMS * 8, 128), F32),
        ],
        compiler_params=pltpu.CompilerParams(vmem_limit_bytes=24 << 20),
        cost_estimate=cost(7),
    )(
        ghosts,
        own_sum,
        total,
        table,
        edges,
        features,
        positions,
        frame,
        w_edge,
        bias,
        w_message,
        w_update,
        w_readout,
        w_heads.T,
    )
    copies = jnp.broadcast_to(part, (frame_count, *part.shape))
    everything = lax.all_to_all(copies, "frame", split_axis=0, concat_axis=0, tiled=True)
    return jnp.sum(everything, axis=0) / frame_count


def solution(mesh):
    placed = (
        P("dom", None),
        P(None, "dom"),
        P("dom", None),
        P("dom"),
        P("dom", None, None),
        P("frame", None, None),
        P(),
        P(),
        P(),
        P(),
        P(),
        P(),
    )
    return jax.shard_map(
        local_step, mesh=mesh, in_specs=placed, out_specs=P(None, "dom"), check_vma=False
    )
```

```python
import jax
import jax.numpy as jnp
from jax import lax
from jax.experimental import pallas as pl
from jax.experimental.pallas import tpu as pltpu
from jax.sharding import PartitionSpec as P

BF = jnp.bfloat16
F32 = jnp.float32
I32 = jnp.int32
message_scale = 0.0884
radial_step = 1.25

ATOMS = 128
HALF = 64
CAP = 64
TABLE = CAP + ATOMS
WIDTH = 512
SLOTS = 128
FEATS = 16
GROUP = 8
GROUPS = HALF // GROUP
EXTRA = 128
PAY = WIDTH + EXTRA
RADIAL = 6
GHOST_ROWS = ((0, 64), (16, 64), (32, 64), (48, 64))
OWN_ROWS = ((0, 64), (0, 96), (0, 112), (0, 128))
TILE = 256


def iota(shape, dim):
    return lax.broadcasted_iota(I32, shape, dim)


def dot(a, b):
    return jnp.dot(a, b, preferred_element_type=F32)


def dot_t(a, b):
    return lax.dot_general(a, b, (((1,), (1,)), ((), ())), preferred_element_type=F32)


def mask(cond):
    return jnp.where(cond, 1.0, 0.0).astype(F32)


def pick(cond):
    return mask(cond).astype(BF)


def parity():
    return lax.axis_index("frame") // (lax.axis_size("frame") // 2)


def local(n):
    return jnp.where(parity() == 1, ATOMS - 1 - n, n)


def entries(ref):
    return [[ref[a, :, c : c + 1] for c in range(3)] for a in range(3)]


def vectors(rot, we_ref, c):
    return 0.5 * (rot[0][c] * we_ref[6:7, :] + rot[1][c] * we_ref[7:8, :] + rot[2][c] * we_ref[8:9, :])


def split(x):
    high = x.astype(BF).astype(F32)
    return high, x - high


def centres(pos_ref):
    atom = local(iota((8, ATOMS), 1))
    in_group = mask(atom // GROUP == iota((8, ATOMS), 0))
    spread = pick(local(iota((ATOMS, ATOMS), 0)) % GROUP == iota((ATOMS, ATOMS), 1) // FEATS)
    return [dot((in_group * pos_ref[c : c + 1, :].astype(F32)).astype(BF), spread) for c in range(3)]


def placed_rows(chosen, pos_ref):
    ones = jnp.ones((ATOMS, ATOMS), BF)
    return [dot((chosen * pos_ref[c : c + 1, :].astype(F32)).astype(BF), ones) for c in range(3)]


def fill_edges(edges, reach, centre, bounds):
    kind = iota((1, ATOMS), 1) % FEATS
    shift = kind.astype(F32) * radial_step
    at = 0
    for g in range(GROUPS):
        lo, hi = bounds[g // 2]
        rel = [reach[c][lo:hi] - centre[c][g : g + 1, :] for c in range(3)]
        dist = jnp.sqrt(rel[0] * rel[0] + rel[1] * rel[1] + rel[2] * rel[2] + 0.25) - shift
        value = jnp.exp(-(dist * dist))
        axis = jnp.where(kind % 3 == 0, rel[0], jnp.where(kind % 3 == 1, rel[1], rel[2]))
        high, low = split(axis)
        axis = jnp.where((kind >= 9) & (kind < 12), low, high)
        value = jnp.where(kind < RADIAL, value, jnp.where(kind < 15, axis, 1.0))
        edges[at : at + hi - lo, :] = value.astype(BF)
        at += hi - lo


def fill_filter(rhs, rot, we_ref, be_ref):
    vec = jnp.concatenate([vectors(rot, we_ref, c) for c in range(3)], axis=0)
    high, low = split(vec)
    rows = jnp.concatenate([0.5 * we_ref[0:RADIAL, :], high, high, low, 0.5 * be_ref[...]], axis=0)
    rows = jnp.concatenate([rows] * GROUP, axis=0).astype(BF)
    block = iota((ATOMS, WIDTH), 0) // FEATS
    for a in range(GROUP):
        rhs[a, :, :] = jnp.where(block == a, rows, jnp.zeros_like(rows))


def fill_times(times, total):
    for a in range(GROUP):
        spread = pick(iota((ATOMS, ATOMS), 0) % HALF == iota((ATOMS, ATOMS), 1) * GROUP + a)
        times[a, :, :] = dot(total, spread)


def sum_rows(prod, rows):
    parts = [prod[r : r + 16] for r in range(0, rows, 16)]
    while len(parts) > SUMS:
        parts = [
            parts[q] + parts[q + 1] if q + 1 < len(parts) else parts[q] for q in range(0, len(parts), 2)
        ]
    total = parts[0].astype(F32)
    for part in parts[1:]:
        total = total + part.astype(F32)
    return total[:8] + total[8:]


SUMS = 2


def offsets_of(bounds):
    offsets = [0]
    for g in range(GROUPS):
        lo, hi = bounds[g // 2]
        offsets.append(offsets[-1] + hi - lo)
    return offsets


OWN_AT = offsets_of(OWN_ROWS)
GHOST_AT = offsets_of(GHOST_ROWS)


def gated(pre):
    half = pre.astype(BF)
    return half * jnp.tanh(half) + half


def cut(rows):
    return [rows[r : r + 16] for r in range(0, rows.shape[0], 16)]


def total_of(parts):
    while len(parts) > SUMS:
        parts = [
            parts[q] + parts[q + 1] if q + 1 < len(parts) else parts[q] for q in range(0, len(parts), 2)
        ]
    total = parts[0].astype(F32)
    for part in parts[1:]:
        total = total + part.astype(F32)
    return total[:8] + total[8:]


def keep(partial, a, k, count, w, done):
    at = pl.multiple_of((a * count + k) * 8, 8)
    for t in range(TILE // 128):
        partial[w * (TILE // 128) + t, pl.ds(at, 8), :] = done[:, t * 128 : (t + 1) * 128]


def collect(partial, rows):
    tiles = []
    for t in range(WIDTH // 128):
        total = partial[t, pl.ds(0, rows, stride=8), :]
        for r in range(1, 8):
            total = total + partial[t, pl.ds(r, rows, stride=8), :]
        tiles.append(total)
    return jnp.concatenate(tiles, axis=1)


def pack_kernel(feat_ref, pos_ref, rows_ref, frame_ref, out_ref):
    wanted = jnp.where(parity() == 1, rows_ref[0, 1:2, :], rows_ref[0, 0:1, :])
    row = iota((CAP, CAP), 0)
    source = jnp.where(parity() == 1, row, CAP - 1 - row)
    column = jnp.sum(
        jnp.where(iota((CAP, CAP), 1) == source, wanted, 0).astype(F32), axis=1, keepdims=True
    ).astype(I32)
    chosen = pick(iota((CAP, ATOMS), 1) == column)
    out_ref[:, :WIDTH] = dot(chosen, feat_ref[...]).astype(BF)
    lane = iota((CAP, EXTRA), 1)
    rest = jnp.zeros((CAP, EXTRA), F32)
    for c in range(3):
        line = chosen.astype(F32) * pos_ref[c : c + 1, :].astype(F32)
        rest = jnp.where(lane == c, jnp.sum(line, axis=1, keepdims=True), rest)
    turn = jnp.zeros((CAP, EXTRA), F32)
    for a in range(3):
        for c in range(3):
            k = 8 + 3 * a + c
            here = (lane == k) | (lane == k + 16) | (lane == k + 32)
            turn = jnp.where(here, frame_ref[a, :, c : c + 1], turn)
    high, rest_of = split(turn)
    mid, low = split(rest_of)
    turn = jnp.where(lane < 24, high, jnp.where(lane < 40, mid, low))
    out_ref[:, WIDTH:] = (rest + turn).astype(BF)


def own_kernel(
    feat_ref,
    pos_ref,
    nbr_ref,
    cnt_ref,
    frame_ref,
    we_ref,
    be_ref,
    wh_ref,
    sum_ref,
    total_ref,
    wh_out,
    table,
    edges,
    rhs,
    times,
    partial,
):
    own = pick(iota((ATOMS, ATOMS), 1) == local(iota((ATOMS, ATOMS), 0)))
    table[...] = dot(own, feat_ref[...]).astype(BF)

    raw = nbr_ref[...]
    order = jnp.where(raw < ATOMS, raw + CAP, jnp.where(raw < ATOMS + CAP, raw - ATOMS, raw))
    order = jnp.where(parity() == 1, 2 * CAP + ATOMS - 1 - order, order)
    by_slot = order.astype(F32).T.astype(BF)
    atom = local(iota((ATOMS, ATOMS), 0))
    lane = iota((ATOMS, ATOMS), 1)
    to_low = pick((atom == lane) & (lane < HALF))
    to_high = pick(atom + HALF == lane)
    folded = dot(by_slot[: SLOTS // 2], to_low) + dot(by_slot[SLOTS // 2 :], to_high)
    cnt = jnp.broadcast_to(cnt_ref[...].astype(F32), (8, ATOMS)).astype(BF)
    live = (dot(cnt, to_low) + dot(cnt, to_high))[0:1, :]
    slot = iota((SLOTS // 2, ATOMS), 0) + jnp.where(iota((SLOTS // 2, ATOMS), 1) < HALF, 0, SLOTS // 2)
    folded = jnp.where(slot.astype(F32) < live, folded, -1.0).astype(BF)
    place = iota((TABLE, ATOMS), 0).astype(F32).astype(BF)
    total = jnp.zeros((TABLE, ATOMS), BF)
    one = jnp.ones((TABLE, ATOMS), BF)
    for k in range(SLOTS // 2):
        total = jnp.where(place == folded[k : k + 1, :], total + one, total)
    total_ref[...] = total
    wh_out[...] = wh_ref[...]
    fill_times(times, total[CAP:])
    fill_edges(edges, placed_rows(own.astype(F32), pos_ref), centres(pos_ref), OWN_ROWS)
    fill_filter(rhs, entries(frame_ref), we_ref, be_ref)

    def step(a, carry):
        share = times[a].astype(BF)
        for w in range(WIDTH // TILE):
            span = slice(w * TILE, (w + 1) * TILE)
            for g in range(GROUPS):
                lo, hi = OWN_ROWS[g // 2]
                weighted = table[lo:hi, span] * share[lo:hi, g : g + 1]
                gate = gated(dot(edges[OWN_AT[g] : OWN_AT[g + 1], :], rhs[a, :, span]))
                keep(partial, a, g, GROUPS, w, total_of(cut(gate * weighted)))
        return carry

    lax.fori_loop(0, GROUP, step, 0)
    sum_ref[...] = collect(partial, HALF)


def last_kernel(
    pay_ref,
    sum_ref,
    total_ref,
    table,
    edges,
    feat_ref,
    pos_ref,
    frame_ref,
    we_ref,
    be_ref,
    wm_ref,
    wu_ref,
    wr_ref,
    wh_ref,
    out_ref,
    ghosts,
    rhs,
    rhs_other,
    times,
    partial,
):
    rot = entries(frame_ref)
    extra = pay_ref[:, WIDTH:]
    head = extra[0:1, :].astype(F32)
    other = []
    for a in range(3):
        other.append([])
        for c in range(3):
            k = 8 + 3 * a + c
            other[a].append(head[:, k : k + 1] + head[:, k + 16 : k + 17] + head[:, k + 32 : k + 33])
    reach = [dot(extra, pick(iota((EXTRA, EXTRA), 0) == c)) for c in range(3)]
    fill_times(times, total_ref[...])
    fill_edges(ghosts, reach, centres(pos_ref), GHOST_ROWS)
    fill_filter(rhs, rot, we_ref, be_ref)
    fill_filter(rhs_other, other, we_ref, be_ref)

    def step(a, carry):
        share = times[a].astype(BF)
        for w in range(WIDTH // TILE):
            span = slice(w * TILE, (w + 1) * TILE)
            near = gated(dot(ghosts[...], rhs[a, :, span]))
            far = gated(dot(ghosts[...], rhs_other[a, :, span]))
            for g in range(GROUPS):
                lo, hi = GHOST_ROWS[g // 2]
                weighted = pay_ref[lo:hi, span] * share[lo:hi, g : g + 1]
                rows = slice(GHOST_AT[g], GHOST_AT[g + 1])
                keep(partial, a, g, 2 * GROUPS, w, total_of(cut(near[rows] * weighted)))
                parts = cut(far[rows] * weighted)
                lo, hi = OWN_ROWS[g // 2]
                weighted = table[lo:hi, span] * share[CAP + lo : CAP + hi, g : g + 1]
                gate = gated(dot(edges[OWN_AT[g] : OWN_AT[g + 1], :], rhs_other[a, :, span]))
                parts = parts + cut(gate * weighted)
                keep(partial, a, GROUPS + g, 2 * GROUPS, w, total_of(parts))
        return carry

    lax.fori_loop(0, GROUP, step, 0)
    total = collect(partial, ATOMS)
    before = [
        piece
        for a in range(GROUP)
        for piece in (sum_ref[a * GROUPS : (a + 1) * GROUPS, :], jnp.zeros((GROUPS, WIDTH), F32))
    ]
    msg = ((total + jnp.concatenate(before, axis=0)) * message_scale).astype(BF)
    row = iota((ATOMS, ATOMS), 0)
    lane = iota((ATOMS, ATOMS), 1)
    row_atom = (row % GROUPS) * GROUP + row // 16
    mine = dot(pick(lane == local(row_atom)), feat_ref[...])

    def silu(x):
        h = 0.5 * x
        return h * jnp.tanh(h) + h

    hidden = silu(dot(msg, wm_ref[...])).astype(BF)
    updated = (mine + dot(hidden, wu_ref[...])).astype(BF)
    readout = silu(dot(updated, wr_ref[...])).astype(BF)
    lane_atom = (lane % GROUPS) * GROUP + lane // 16
    out = jnp.zeros((4, ATOMS), F32)
    for f, turn in enumerate((rot, other)):
        back = pick((local(row) == lane_atom) & ((lane // GROUPS) % 2 == f))
        heads = dot_t(wh_ref[...], dot(back, readout).astype(BF))
        force = [
            turn[0][c] * heads[0:1] + turn[1][c] * heads[1:2] + turn[2][c] * heads[2:3] for c in range(3)
        ]
        out = out + jnp.concatenate(force + [heads[3:4]], axis=0)
    out_ref[...] = out


def cost(microseconds):
    return pl.CostEstimate(flops=microseconds * 10**9, bytes_accessed=microseconds * 10**6, transcendentals=0)


def local_step(
    features,
    positions,
    neighbours,
    counts,
    send_rows,
    frames,
    w_edge,
    b_edge,
    w_message,
    w_update,
    w_readout,
    w_heads,
):
    dom_count = lax.axis_size("dom")
    frame_count = lax.axis_size("frame")
    frame = jnp.transpose(frames, (1, 0, 2))
    payload = pl.pallas_call(
        pack_kernel,
        out_shape=jax.ShapeDtypeStruct((CAP, PAY), BF),
        cost_estimate=cost(2),
    )(features, positions, send_rows, frame)
    pairs = []
    for d in range(dom_count):
        for f in range(frame_count):
            to = (d + 1) % dom_count if f >= frame_count // 2 else (d - 1) % dom_count
            pairs.append((d * frame_count + f, to * frame_count + (f + frame_count // 2) % frame_count))
    ghosts = lax.ppermute(payload, ("dom", "frame"), pairs)
    bias = b_edge.reshape(1, WIDTH)
    own_sum, total, heads, table, edges = pl.pallas_call(
        own_kernel,
        out_shape=[
            jax.ShapeDtypeStruct((HALF, WIDTH), F32),
            jax.ShapeDtypeStruct((TABLE, ATOMS), BF),
            jax.ShapeDtypeStruct((4, WIDTH), BF),
            jax.ShapeDtypeStruct((ATOMS, WIDTH), BF),
            jax.ShapeDtypeStruct((OWN_AT[-1], ATOMS), BF),
        ],
        scratch_shapes=[
            pltpu.VMEM((GROUP, ATOMS, WIDTH), BF),
            pltpu.VMEM((GROUP, ATOMS, ATOMS), F32),
            pltpu.VMEM((WIDTH // 128, HALF * 8, 128), F32),
        ],
        compiler_params=pltpu.CompilerParams(vmem_limit_bytes=24 << 20),
        cost_estimate=cost(5),
    )(features, positions, neighbours, counts.reshape(1, ATOMS), frame, w_edge, bias, w_heads.T)
    part = pl.pallas_call(
        last_kernel,
        out_shape=jax.ShapeDtypeStruct((4, ATOMS), F32),
        scratch_shapes=[
            pltpu.VMEM((GHOST_AT[-1], ATOMS), BF),
            pltpu.VMEM((GROUP, ATOMS, WIDTH), BF),
            pltpu.VMEM((GROUP, ATOMS, WIDTH), BF),
            pltpu.VMEM((GROUP, TABLE, ATOMS), F32),
            pltpu.VMEM((WIDTH // 128, ATOMS * 8, 128), F32),
        ],
        compiler_params=pltpu.CompilerParams(vmem_limit_bytes=24 << 20),
        cost_estimate=cost(7),
    )(
        ghosts,
        own_sum,
        total,
        table,
        edges,
        features,
        positions,
        frame,
        w_edge,
        bias,
        w_message,
        w_update,
        w_readout,
        heads,
    )
    copies = jnp.broadcast_to(part, (frame_count, *part.shape))
    everything = lax.all_to_all(copies, "frame", split_axis=0, concat_axis=0, tiled=True)
    return jnp.sum(everything, axis=0) / frame_count


def solution(mesh):
    placed = (
        P("dom", None),
        P(None, "dom"),
        P("dom", None),
        P("dom"),
        P("dom", None, None),
        P("frame", None, None),
        P(),
        P(),
        P(),
        P(),
        P(),
        P(),
    )
    return jax.shard_map(
        local_step, mesh=mesh, in_specs=placed, out_specs=P(None, "dom"), check_vma=False
    )
```

```python
import jax
import jax.numpy as jnp
from jax import lax
from jax.experimental import pallas as pl
from jax.experimental.pallas import tpu as pltpu
from jax.sharding import PartitionSpec as P

BF = jnp.bfloat16
F32 = jnp.float32
I32 = jnp.int32
message_scale = 0.0884
radial_step = 1.25

ATOMS = 128
HALF = 64
CAP = 64
TABLE = CAP + ATOMS
WIDTH = 512
SLOTS = 128
FEATS = 16
GROUP = 8
GROUPS = HALF // GROUP
EXTRA = 128
PAY = WIDTH + EXTRA
RADIAL = 6
GHOST_ROWS = ((0, 64), (16, 64), (32, 64), (48, 64))
OWN_ROWS = ((0, 64), (0, 96), (0, 112), (0, 128))
TILE = 256


def iota(shape, dim):
    return lax.broadcasted_iota(I32, shape, dim)


def dot(a, b):
    return jnp.dot(a, b, preferred_element_type=F32)


def dot_t(a, b):
    return lax.dot_general(a, b, (((1,), (1,)), ((), ())), preferred_element_type=F32)


def mask(cond):
    return jnp.where(cond, 1.0, 0.0).astype(F32)


def pick(cond):
    return mask(cond).astype(BF)


def parity():
    return lax.axis_index("frame") // (lax.axis_size("frame") // 2)


def local(n):
    return jnp.where(parity() == 1, ATOMS - 1 - n, n)


def entries(ref):
    return [[ref[a, :, c : c + 1] for c in range(3)] for a in range(3)]


def vectors(rot, we_ref, c):
    return 0.5 * (rot[0][c] * we_ref[6:7, :] + rot[1][c] * we_ref[7:8, :] + rot[2][c] * we_ref[8:9, :])


def split(x):
    high = x.astype(BF).astype(F32)
    return high, x - high


def centres(pos_ref):
    atom = local(iota((8, ATOMS), 1))
    in_group = mask(atom // GROUP == iota((8, ATOMS), 0))
    spread = pick(local(iota((ATOMS, ATOMS), 0)) % GROUP == iota((ATOMS, ATOMS), 1) // FEATS)
    return [dot((in_group * pos_ref[c : c + 1, :].astype(F32)).astype(BF), spread) for c in range(3)]


def placed_rows(chosen, pos_ref):
    ones = jnp.ones((ATOMS, ATOMS), BF)
    return [dot((chosen * pos_ref[c : c + 1, :].astype(F32)).astype(BF), ones) for c in range(3)]


def fill_edges(edges, reach, centre, bounds):
    kind = iota((1, ATOMS), 1) % FEATS
    shift = kind.astype(F32) * radial_step
    at = 0
    for g in range(GROUPS):
        lo, hi = bounds[g // 2]
        rel = [reach[c][lo:hi] - centre[c][g : g + 1, :] for c in range(3)]
        dist = jnp.sqrt(rel[0] * rel[0] + rel[1] * rel[1] + rel[2] * rel[2] + 0.25) - shift
        value = jnp.exp(-(dist * dist))
        axis = jnp.where(kind % 3 == 0, rel[0], jnp.where(kind % 3 == 1, rel[1], rel[2]))
        high, low = split(axis)
        axis = jnp.where((kind >= 9) & (kind < 12), low, high)
        value = jnp.where(kind < RADIAL, value, jnp.where(kind < 15, axis, 1.0))
        edges[at : at + hi - lo, :] = value.astype(BF)
        at += hi - lo


def fill_filter(rhs, rot, we_ref, be_ref):
    vec = jnp.concatenate([vectors(rot, we_ref, c) for c in range(3)], axis=0)
    high, low = split(vec)
    rows = jnp.concatenate([0.5 * we_ref[0:RADIAL, :], high, high, low, 0.5 * be_ref[...]], axis=0)
    rows = jnp.concatenate([rows] * GROUP, axis=0).astype(BF)
    block = iota((ATOMS, WIDTH), 0) // FEATS
    for a in range(GROUP):
        rhs[a, :, :] = jnp.where(block == a, rows, jnp.zeros_like(rows))


def fill_times(times, total):
    for a in range(GROUP):
        spread = pick(iota((ATOMS, ATOMS), 0) % HALF == iota((ATOMS, ATOMS), 1) * GROUP + a)
        times[a, :, :] = dot(total, spread).astype(BF)


def sum_rows(prod, rows):
    parts = [prod[r : r + 16] for r in range(0, rows, 16)]
    while len(parts) > SUMS:
        parts = [
            parts[q] + parts[q + 1] if q + 1 < len(parts) else parts[q] for q in range(0, len(parts), 2)
        ]
    total = parts[0].astype(F32)
    for part in parts[1:]:
        total = total + part.astype(F32)
    return total[:8] + total[8:]


SUMS = 1


def offsets_of(bounds):
    offsets = [0]
    for g in range(GROUPS):
        lo, hi = bounds[g // 2]
        offsets.append(offsets[-1] + hi - lo)
    return offsets


OWN_AT = offsets_of(OWN_ROWS)
GHOST_AT = offsets_of(GHOST_ROWS)


def gated(pre):
    half = pre.astype(BF)
    return half * jnp.tanh(half) + half


def cut(rows):
    return [rows[r : r + 16] for r in range(0, rows.shape[0], 16)]


def total_of(parts):
    while len(parts) > SUMS:
        parts = [
            parts[q] + parts[q + 1] if q + 1 < len(parts) else parts[q] for q in range(0, len(parts), 2)
        ]
    total = parts[0].astype(F32)
    for part in parts[1:]:
        total = total + part.astype(F32)
    return total[:8] + total[8:]


def keep(partial, a, k, count, w, done):
    at = pl.multiple_of((a * count + k) * 8, 8)
    for t in range(TILE // 128):
        partial[w * (TILE // 128) + t, pl.ds(at, 8), :] = done[:, t * 128 : (t + 1) * 128]


def collect(partial, rows):
    tiles = []
    for t in range(WIDTH // 128):
        total = partial[t, pl.ds(0, rows, stride=8), :]
        for r in range(1, 8):
            total = total + partial[t, pl.ds(r, rows, stride=8), :]
        tiles.append(total)
    return jnp.concatenate(tiles, axis=1)


def early():
    return lax.axis_index("dom") == 0


def sum_own(table, edges, rhs, times, partial, sum_ref):
    def step(a, carry):
        share = times[a]
        for w in range(WIDTH // TILE):
            span = slice(w * TILE, (w + 1) * TILE)
            for first in range(0, GROUPS, 2):
                pre = dot(edges[OWN_AT[first] : OWN_AT[first + 2], :], rhs[a, :, span]).astype(BF)
                for g in range(first, first + 2):
                    lo, hi = OWN_ROWS[g // 2]
                    weighted = table[lo:hi, span] * share[lo:hi, g : g + 1]
                    gate = gated(pre[OWN_AT[g] - OWN_AT[first] : OWN_AT[g + 1] - OWN_AT[first]])
                    keep(partial, a, g, GROUPS, w, total_of(cut(gate * weighted)))
        return carry

    lax.fori_loop(0, GROUP, step, 0)
    sum_ref[...] = collect(partial, HALF)


def first_kernel(
    feat_ref,
    pos_ref,
    rows_ref,
    frame_ref,
    nbr_ref,
    cnt_ref,
    we_ref,
    be_ref,
    wh_ref,
    pay_ref,
    sum_ref,
    total_ref,
    table,
    edges,
    rhs,
    times,
    pos_out,
    frame_out,
    we_out,
    be_out,
    wh_out,
    partial,
):
    pos_out[...] = pos_ref[...]
    frame_out[...] = frame_ref[...]
    we_out[...] = we_ref[...]
    be_out[...] = be_ref[...]
    wh_out[...] = wh_ref[...]
    wanted = jnp.where(parity() == 1, rows_ref[0, 1:2, :], rows_ref[0, 0:1, :])
    row = iota((CAP, CAP), 0)
    source = jnp.where(parity() == 1, row, CAP - 1 - row)
    column = jnp.sum(
        jnp.where(iota((CAP, CAP), 1) == source, wanted, 0).astype(F32), axis=1, keepdims=True
    ).astype(I32)
    chosen = pick(iota((CAP, ATOMS), 1) == column)
    pay_ref[:, :WIDTH] = dot(chosen, feat_ref[...]).astype(BF)
    lane = iota((CAP, EXTRA), 1)
    rest = jnp.zeros((CAP, EXTRA), F32)
    for c in range(3):
        line = chosen.astype(F32) * pos_ref[c : c + 1, :].astype(F32)
        rest = jnp.where(lane == c, jnp.sum(line, axis=1, keepdims=True), rest)
    turn = jnp.zeros((CAP, EXTRA), F32)
    for a in range(3):
        for c in range(3):
            k = 8 + 3 * a + c
            here = (lane == k) | (lane == k + 16) | (lane == k + 32)
            turn = jnp.where(here, frame_ref[a, :, c : c + 1], turn)
    high, rest_of = split(turn)
    mid, low = split(rest_of)
    turn = jnp.where(lane < 24, high, jnp.where(lane < 40, mid, low))
    pay_ref[:, WIDTH:] = (rest + turn).astype(BF)

    own = pick(iota((ATOMS, ATOMS), 1) == local(iota((ATOMS, ATOMS), 0)))
    table[...] = dot(own, feat_ref[...]).astype(BF)

    raw = nbr_ref[...]
    order = jnp.where(raw < ATOMS, raw + CAP, jnp.where(raw < ATOMS + CAP, raw - ATOMS, raw))
    order = jnp.where(parity() == 1, 2 * CAP + ATOMS - 1 - order, order)
    by_slot = order.astype(F32).T.astype(BF)
    atom = local(iota((ATOMS, ATOMS), 0))
    lane = iota((ATOMS, ATOMS), 1)
    to_low = pick((atom == lane) & (lane < HALF))
    to_high = pick(atom + HALF == lane)
    folded = dot(by_slot[: SLOTS // 2], to_low) + dot(by_slot[SLOTS // 2 :], to_high)
    cnt = jnp.broadcast_to(cnt_ref[...].astype(F32), (8, ATOMS)).astype(BF)
    live = (dot(cnt, to_low) + dot(cnt, to_high))[0:1, :]
    slot = iota((SLOTS // 2, ATOMS), 0) + jnp.where(iota((SLOTS // 2, ATOMS), 1) < HALF, 0, SLOTS // 2)
    folded = jnp.where(slot.astype(F32) < live, folded, -1.0).astype(BF)
    place = iota((TABLE, ATOMS), 0).astype(F32).astype(BF)
    total = jnp.zeros((TABLE, ATOMS), BF)
    one = jnp.ones((TABLE, ATOMS), BF)
    for k in range(SLOTS // 2):
        total = jnp.where(place == folded[k : k + 1, :], total + one, total)
    total_ref[...] = total
    fill_times(times, total[CAP:])
    fill_edges(edges, placed_rows(own.astype(F32), pos_ref), centres(pos_ref), OWN_ROWS)
    fill_filter(rhs, entries(frame_ref), we_ref, be_ref)

    @pl.when(early())
    def _():
        sum_own(table, edges, rhs, times, partial, sum_ref)


def own_kernel(before_ref, table, edges, rhs, times, sum_ref, partial):
    @pl.when(early())
    def _():
        sum_ref[...] = before_ref[...]

    @pl.when(jnp.logical_not(early()))
    def _():
        sum_own(table, edges, rhs, times, partial, sum_ref)


def last_kernel(
    pay_ref,
    sum_ref,
    total_ref,
    table,
    edges,
    rhs,
    own_times,
    pos_ref,
    frame_ref,
    we_ref,
    be_ref,
    wm_ref,
    wu_ref,
    wr_ref,
    wh_ref,
    out_ref,
    ghosts,
    rhs_other,
    times,
    partial,
):
    rot = entries(frame_ref)
    extra = pay_ref[:, WIDTH:]
    head = extra[0:1, :].astype(F32)
    other = []
    for a in range(3):
        other.append([])
        for c in range(3):
            k = 8 + 3 * a + c
            other[a].append(head[:, k : k + 1] + head[:, k + 16 : k + 17] + head[:, k + 32 : k + 33])
    reach = [dot(extra, pick(iota((EXTRA, EXTRA), 0) == c)) for c in range(3)]
    fill_times(times, total_ref[:CAP, :])
    fill_edges(ghosts, reach, centres(pos_ref), GHOST_ROWS)
    fill_filter(rhs_other, other, we_ref, be_ref)

    def step(a, carry):
        share = times[a]
        own_share = own_times[a]
        for w in range(WIDTH // TILE):
            span = slice(w * TILE, (w + 1) * TILE)
            near = gated(dot(ghosts[...], rhs[a, :, span]))
            far = gated(dot(ghosts[...], rhs_other[a, :, span]))
            for first in range(0, GROUPS, 2):
                pre = dot(edges[OWN_AT[first] : OWN_AT[first + 2], :], rhs_other[a, :, span]).astype(BF)
                for g in range(first, first + 2):
                    lo, hi = GHOST_ROWS[g // 2]
                    weighted = pay_ref[lo:hi, span] * share[lo:hi, g : g + 1]
                    rows = slice(GHOST_AT[g], GHOST_AT[g + 1])
                    keep(partial, a, g, 2 * GROUPS, w, total_of(cut(near[rows] * weighted)))
                    parts = cut(far[rows] * weighted)
                    lo, hi = OWN_ROWS[g // 2]
                    weighted = table[lo:hi, span] * own_share[lo:hi, g : g + 1]
                    gate = gated(pre[OWN_AT[g] - OWN_AT[first] : OWN_AT[g + 1] - OWN_AT[first]])
                    parts = parts + cut(gate * weighted)
                    keep(partial, a, GROUPS + g, 2 * GROUPS, w, total_of(parts))
        return carry

    lax.fori_loop(0, GROUP, step, 0)
    total = collect(partial, ATOMS)
    before = [
        piece
        for a in range(GROUP)
        for piece in (sum_ref[a * GROUPS : (a + 1) * GROUPS, :], jnp.zeros((GROUPS, WIDTH), F32))
    ]
    msg = ((total + jnp.concatenate(before, axis=0)) * message_scale).astype(BF)
    row = iota((ATOMS, ATOMS), 0)
    lane = iota((ATOMS, ATOMS), 1)
    row_atom = (row % GROUPS) * GROUP + row // 16
    mine = dot(pick(lane == row_atom), table[...])

    def silu(x):
        h = 0.5 * x
        return h * jnp.tanh(h) + h

    hidden = silu(dot(msg, wm_ref[...])).astype(BF)
    updated = (mine + dot(hidden, wu_ref[...])).astype(BF)
    readout = silu(dot(updated, wr_ref[...])).astype(BF)
    lane_atom = (lane % GROUPS) * GROUP + lane // 16
    out = jnp.zeros((4, ATOMS), F32)
    for f, turn in enumerate((rot, other)):
        back = pick((local(row) == lane_atom) & ((lane // GROUPS) % 2 == f))
        heads = dot_t(wh_ref[...], dot(back, readout).astype(BF))
        force = [
            turn[0][c] * heads[0:1] + turn[1][c] * heads[1:2] + turn[2][c] * heads[2:3] for c in range(3)
        ]
        out = out + jnp.concatenate(force + [heads[3:4]], axis=0)
    out_ref[...] = out


def cost(microseconds):
    return pl.CostEstimate(flops=microseconds * 10**9, bytes_accessed=microseconds * 10**6, transcendentals=0)


def local_step(
    features,
    positions,
    neighbours,
    counts,
    send_rows,
    frames,
    w_edge,
    b_edge,
    w_message,
    w_update,
    w_readout,
    w_heads,
):
    dom_count = lax.axis_size("dom")
    frame_count = lax.axis_size("frame")
    frame = jnp.transpose(frames, (1, 0, 2))
    bias = b_edge.reshape(1, WIDTH)
    direct = [
        pltpu.with_memory_space_constraint(x, pltpu.MemorySpace.HBM)
        for x in (
            features,
            positions,
            send_rows,
            frame,
            neighbours,
            counts.reshape(1, ATOMS),
            w_edge,
            bias,
            w_heads.T,
        )
    ]
    payload, before, total, table, edges, rhs, times, *small, heads = pl.pallas_call(
        first_kernel,
        out_shape=[
            pltpu.VMEM((CAP, PAY), BF),
            pltpu.VMEM((HALF, WIDTH), F32),
            pltpu.VMEM((TABLE, ATOMS), BF),
            pltpu.VMEM((ATOMS, WIDTH), BF),
            pltpu.VMEM((OWN_AT[-1], ATOMS), BF),
            pltpu.VMEM((GROUP, ATOMS, WIDTH), BF),
            pltpu.VMEM((GROUP, ATOMS, ATOMS), BF),
            pltpu.VMEM(positions.shape, BF),
            pltpu.VMEM(frame.shape, F32),
            pltpu.VMEM(w_edge.shape, F32),
            pltpu.VMEM(bias.shape, F32),
            pltpu.VMEM((4, WIDTH), BF),
        ],
        scratch_shapes=[pltpu.VMEM((WIDTH // 128, HALF * 8, 128), F32)],
        compiler_params=pltpu.CompilerParams(vmem_limit_bytes=24 << 20),
        cost_estimate=cost(3),
    )(*direct)
    pairs = []
    for d in range(dom_count):
        for f in range(frame_count):
            to = (d + 1) % dom_count if f >= frame_count // 2 else (d - 1) % dom_count
            pairs.append((d * frame_count + f, to * frame_count + (f + frame_count // 2) % frame_count))
    ghosts = lax.ppermute(payload, ("dom", "frame"), pairs)
    own_sum = pl.pallas_call(
        own_kernel,
        out_shape=pltpu.VMEM((HALF, WIDTH), F32),
        scratch_shapes=[pltpu.VMEM((WIDTH // 128, HALF * 8, 128), F32)],
        compiler_params=pltpu.CompilerParams(vmem_limit_bytes=24 << 20),
        cost_estimate=cost(4),
    )(before, table, edges, rhs, times)
    part = pl.pallas_call(
        last_kernel,
        out_shape=jax.ShapeDtypeStruct((4, ATOMS), F32),
        scratch_shapes=[
            pltpu.VMEM((GHOST_AT[-1], ATOMS), BF),
            pltpu.VMEM((GROUP, ATOMS, WIDTH), BF),
            pltpu.VMEM((GROUP, CAP, ATOMS), BF),
            pltpu.VMEM((WIDTH // 128, ATOMS * 8, 128), F32),
        ],
        compiler_params=pltpu.CompilerParams(vmem_limit_bytes=24 << 20),
        cost_estimate=cost(7),
    )(
        ghosts,
        own_sum,
        total,
        table,
        edges,
        rhs,
        times,
        *small,
        w_message,
        w_update,
        w_readout,
        heads,
    )
    copies = jnp.broadcast_to(part, (frame_count, *part.shape))
    everything = lax.all_to_all(copies, "frame", split_axis=0, concat_axis=0, tiled=True)
    return jnp.sum(everything, axis=0) / frame_count


def solution(mesh):
    placed = (
        P("dom", None),
        P(None, "dom"),
        P("dom", None),
        P("dom"),
        P("dom", None, None),
        P("frame", None, None),
        P(),
        P(),
        P(),
        P(),
        P(),
        P(),
    )
    return jax.shard_map(
        local_step, mesh=mesh, in_specs=placed, out_specs=P(None, "dom"), check_vma=False
    )
```

```python
import jax
import jax.numpy as jnp
from jax import lax
from jax.experimental import pallas as pl
from jax.experimental.pallas import tpu as pltpu
from jax.sharding import PartitionSpec as P

BF = jnp.bfloat16
F32 = jnp.float32
I32 = jnp.int32
message_scale = 0.0884
radial_step = 1.25

ATOMS = 128
HALF = 64
CAP = 64
TABLE = CAP + ATOMS
WIDTH = 512
SLOTS = 128
FEATS = 16
GROUP = 8
GROUPS = HALF // GROUP
EXTRA = 128
PAY = WIDTH + EXTRA
RADIAL = 6
GHOST_ROWS = ((0, 64), (16, 64), (32, 64), (48, 64))
OWN_ROWS = ((0, 64), (0, 96), (0, 112), (0, 128))
TILE = 256


def iota(shape, dim):
    return lax.broadcasted_iota(I32, shape, dim)


def dot(a, b):
    return jnp.dot(a, b, preferred_element_type=F32)


def dot_t(a, b):
    return lax.dot_general(a, b, (((1,), (1,)), ((), ())), preferred_element_type=F32)


def mask(cond):
    return jnp.where(cond, 1.0, 0.0).astype(F32)


def pick(cond):
    return mask(cond).astype(BF)


def parity():
    return lax.axis_index("frame") // (lax.axis_size("frame") // 2)


def local(n):
    return jnp.where(parity() == 1, ATOMS - 1 - n, n)


def entries(ref):
    return [[ref[a, :, c : c + 1] for c in range(3)] for a in range(3)]


def vectors(rot, we_ref, c):
    return 0.5 * (rot[0][c] * we_ref[6:7, :] + rot[1][c] * we_ref[7:8, :] + rot[2][c] * we_ref[8:9, :])


def split(x):
    high = x.astype(BF).astype(F32)
    return high, x - high


def centres(pos_ref):
    atom = local(iota((8, ATOMS), 1))
    in_group = mask(atom // GROUP == iota((8, ATOMS), 0))
    spread = pick(local(iota((ATOMS, ATOMS), 0)) % GROUP == iota((ATOMS, ATOMS), 1) // FEATS)
    return [dot((in_group * pos_ref[c : c + 1, :].astype(F32)).astype(BF), spread) for c in range(3)]


def placed_rows(chosen, pos_ref):
    ones = jnp.ones((ATOMS, ATOMS), BF)
    return [dot((chosen * pos_ref[c : c + 1, :].astype(F32)).astype(BF), ones) for c in range(3)]


def fill_edges(edges, reach, centre, bounds):
    kind = iota((1, ATOMS), 1) % FEATS
    shift = kind.astype(F32) * radial_step
    at = 0
    for g in range(GROUPS):
        lo, hi = bounds[g // 2]
        rel = [reach[c][lo:hi] - centre[c][g : g + 1, :] for c in range(3)]
        dist = jnp.sqrt(rel[0] * rel[0] + rel[1] * rel[1] + rel[2] * rel[2] + 0.25) - shift
        value = jnp.exp(-(dist * dist))
        axis = jnp.where(kind % 3 == 0, rel[0], jnp.where(kind % 3 == 1, rel[1], rel[2]))
        high, low = split(axis)
        axis = jnp.where((kind >= 9) & (kind < 12), low, high)
        value = jnp.where(kind < RADIAL, value, jnp.where(kind < 15, axis, 1.0))
        edges[at : at + hi - lo, :] = value.astype(BF)
        at += hi - lo


def fill_filter(rhs, rot, we_ref, be_ref):
    vec = jnp.concatenate([vectors(rot, we_ref, c) for c in range(3)], axis=0)
    high, low = split(vec)
    rows = jnp.concatenate([0.5 * we_ref[0:RADIAL, :], high, high, low, 0.5 * be_ref[...]], axis=0)
    rows = jnp.concatenate([rows] * GROUP, axis=0).astype(BF)
    block = iota((ATOMS, WIDTH), 0) // FEATS
    for a in range(GROUP):
        rhs[a, :, :] = jnp.where(block == a, rows, jnp.zeros_like(rows))


def fill_times(times, total):
    for a in range(GROUP):
        spread = pick(iota((ATOMS, ATOMS), 0) % HALF == iota((ATOMS, ATOMS), 1) * GROUP + a)
        times[a, :, :] = dot(total, spread).astype(BF)


def sum_rows(prod, rows):
    parts = [prod[r : r + 16] for r in range(0, rows, 16)]
    while len(parts) > SUMS:
        parts = [
            parts[q] + parts[q + 1] if q + 1 < len(parts) else parts[q] for q in range(0, len(parts), 2)
        ]
    total = parts[0].astype(F32)
    for part in parts[1:]:
        total = total + part.astype(F32)
    return total[:8] + total[8:]


SUMS = 1


def offsets_of(bounds):
    offsets = [0]
    for g in range(GROUPS):
        lo, hi = bounds[g // 2]
        offsets.append(offsets[-1] + hi - lo)
    return offsets


OWN_AT = offsets_of(OWN_ROWS)
GHOST_AT = offsets_of(GHOST_ROWS)


def gated(pre):
    half = pre.astype(BF)
    return half * jnp.tanh(half) + half


def cut(rows):
    return [rows[r : r + 16] for r in range(0, rows.shape[0], 16)]


def total_of(parts):
    while len(parts) > SUMS:
        parts = [
            parts[q] + parts[q + 1] if q + 1 < len(parts) else parts[q] for q in range(0, len(parts), 2)
        ]
    total = parts[0].astype(F32)
    for part in parts[1:]:
        total = total + part.astype(F32)
    return total[:8] + total[8:]


def keep(partial, a, k, count, w, done):
    at = pl.multiple_of((a * count + k) * 8, 8)
    for t in range(TILE // 128):
        partial[w * (TILE // 128) + t, pl.ds(at, 8), :] = done[:, t * 128 : (t + 1) * 128]


def collect(partial, rows):
    tiles = []
    for t in range(WIDTH // 128):
        total = partial[t, pl.ds(0, rows, stride=8), :]
        for r in range(1, 8):
            total = total + partial[t, pl.ds(r, rows, stride=8), :]
        tiles.append(total)
    return jnp.concatenate(tiles, axis=1)


def early():
    return (lax.axis_index("dom") == 0) & (parity() == 0)


def sum_own(table, edges, rhs, times, partial, sum_ref):
    def step(a, carry):
        share = times[a]
        for w in range(WIDTH // TILE):
            span = slice(w * TILE, (w + 1) * TILE)
            for first in range(0, GROUPS, 2):
                pre = dot(edges[OWN_AT[first] : OWN_AT[first + 2], :], rhs[a, :, span]).astype(BF)
                for g in range(first, first + 2):
                    lo, hi = OWN_ROWS[g // 2]
                    weighted = table[lo:hi, span] * share[lo:hi, g : g + 1]
                    gate = gated(pre[OWN_AT[g] - OWN_AT[first] : OWN_AT[g + 1] - OWN_AT[first]])
                    keep(partial, a, g, GROUPS, w, total_of(cut(gate * weighted)))
        return carry

    lax.fori_loop(0, GROUP, step, 0)
    sum_ref[...] = collect(partial, HALF)


def prepare_and_sum(
    feat_ref,
    pos_ref,
    frame_ref,
    nbr_ref,
    cnt_ref,
    we_ref,
    be_ref,
    sum_ref,
    total_ref,
    table,
    edges,
    rhs,
    times,
    partial,
):
    own = pick(iota((ATOMS, ATOMS), 1) == local(iota((ATOMS, ATOMS), 0)))
    table[...] = dot(own, feat_ref[...]).astype(BF)

    raw = nbr_ref[...]
    order = jnp.where(raw < ATOMS, raw + CAP, jnp.where(raw < ATOMS + CAP, raw - ATOMS, raw))
    order = jnp.where(parity() == 1, 2 * CAP + ATOMS - 1 - order, order)
    by_slot = order.astype(F32).T.astype(BF)
    atom = local(iota((ATOMS, ATOMS), 0))
    lane = iota((ATOMS, ATOMS), 1)
    to_low = pick((atom == lane) & (lane < HALF))
    to_high = pick(atom + HALF == lane)
    folded = dot(by_slot[: SLOTS // 2], to_low) + dot(by_slot[SLOTS // 2 :], to_high)
    cnt = jnp.broadcast_to(cnt_ref[...].astype(F32), (8, ATOMS)).astype(BF)
    live = (dot(cnt, to_low) + dot(cnt, to_high))[0:1, :]
    slot = iota((SLOTS // 2, ATOMS), 0) + jnp.where(iota((SLOTS // 2, ATOMS), 1) < HALF, 0, SLOTS // 2)
    folded = jnp.where(slot.astype(F32) < live, folded, -1.0).astype(BF)
    place = iota((TABLE, ATOMS), 0).astype(F32).astype(BF)
    total = jnp.zeros((TABLE, ATOMS), BF)
    one = jnp.ones((TABLE, ATOMS), BF)
    for k in range(SLOTS // 2):
        total = jnp.where(place == folded[k : k + 1, :], total + one, total)
    total_ref[...] = total
    fill_times(times, total[CAP:])
    fill_edges(edges, placed_rows(own.astype(F32), pos_ref), centres(pos_ref), OWN_ROWS)
    fill_filter(rhs, entries(frame_ref), we_ref, be_ref)
    sum_own(table, edges, rhs, times, partial, sum_ref)


def first_kernel(rows_ref, *refs):
    sources, (pay_ref,), results, partial = refs[:8], refs[8:9], refs[9:23], refs[23]
    for source, result in zip(sources, results[:8]):
        result[...] = source[...]
    feat_ref, pos_ref, frame_ref = sources[:3]
    wanted = jnp.where(parity() == 1, rows_ref[0, 1:2, :], rows_ref[0, 0:1, :])
    row = iota((CAP, CAP), 0)
    source = jnp.where(parity() == 1, row, CAP - 1 - row)
    column = jnp.sum(
        jnp.where(iota((CAP, CAP), 1) == source, wanted, 0).astype(F32), axis=1, keepdims=True
    ).astype(I32)
    chosen = pick(iota((CAP, ATOMS), 1) == column)
    pay_ref[:, :WIDTH] = dot(chosen, feat_ref[...]).astype(BF)
    lane = iota((CAP, EXTRA), 1)
    rest = jnp.zeros((CAP, EXTRA), F32)
    for c in range(3):
        line = chosen.astype(F32) * pos_ref[c : c + 1, :].astype(F32)
        rest = jnp.where(lane == c, jnp.sum(line, axis=1, keepdims=True), rest)
    turn = jnp.zeros((CAP, EXTRA), F32)
    for a in range(3):
        for c in range(3):
            k = 8 + 3 * a + c
            here = (lane == k) | (lane == k + 16) | (lane == k + 32)
            turn = jnp.where(here, frame_ref[a, :, c : c + 1], turn)
    high, rest_of = split(turn)
    mid, low = split(rest_of)
    turn = jnp.where(lane < 24, high, jnp.where(lane < 40, mid, low))
    pay_ref[:, WIDTH:] = (rest + turn).astype(BF)

    @pl.when(early())
    def _():
        prepare_and_sum(*sources[:7], *results[8:], partial)


def own_kernel(*refs):
    sources, before, results, partial = refs[:7], refs[7:13], refs[13:19], refs[19]

    @pl.when(early())
    def _():
        for source, result in zip(before, results):
            result[...] = source[...]

    @pl.when(jnp.logical_not(early()))
    def _():
        prepare_and_sum(*sources, *results, partial)


def last_kernel(
    pay_ref,
    sum_ref,
    total_ref,
    table,
    edges,
    rhs,
    own_times,
    pos_ref,
    frame_ref,
    we_ref,
    be_ref,
    wm_ref,
    wu_ref,
    wr_ref,
    wh_ref,
    out_ref,
    ghosts,
    rhs_other,
    times,
    partial,
):
    rot = entries(frame_ref)
    extra = pay_ref[:, WIDTH:]
    head = extra[0:1, :].astype(F32)
    other = []
    for a in range(3):
        other.append([])
        for c in range(3):
            k = 8 + 3 * a + c
            other[a].append(head[:, k : k + 1] + head[:, k + 16 : k + 17] + head[:, k + 32 : k + 33])
    reach = [dot(extra, pick(iota((EXTRA, EXTRA), 0) == c)) for c in range(3)]
    fill_times(times, total_ref[:CAP, :])
    fill_edges(ghosts, reach, centres(pos_ref), GHOST_ROWS)
    fill_filter(rhs_other, other, we_ref, be_ref)

    def step(a, carry):
        share = times[a]
        own_share = own_times[a]
        for w in range(WIDTH // TILE):
            span = slice(w * TILE, (w + 1) * TILE)
            near = gated(dot(ghosts[...], rhs[a, :, span]))
            far = gated(dot(ghosts[...], rhs_other[a, :, span]))
            for first in range(0, GROUPS, 2):
                pre = dot(edges[OWN_AT[first] : OWN_AT[first + 2], :], rhs_other[a, :, span]).astype(BF)
                for g in range(first, first + 2):
                    lo, hi = GHOST_ROWS[g // 2]
                    weighted = pay_ref[lo:hi, span] * share[lo:hi, g : g + 1]
                    rows = slice(GHOST_AT[g], GHOST_AT[g + 1])
                    keep(partial, a, g, 2 * GROUPS, w, total_of(cut(near[rows] * weighted)))
                    parts = cut(far[rows] * weighted)
                    lo, hi = OWN_ROWS[g // 2]
                    weighted = table[lo:hi, span] * own_share[lo:hi, g : g + 1]
                    gate = gated(pre[OWN_AT[g] - OWN_AT[first] : OWN_AT[g + 1] - OWN_AT[first]])
                    parts = parts + cut(gate * weighted)
                    keep(partial, a, GROUPS + g, 2 * GROUPS, w, total_of(parts))
        return carry

    lax.fori_loop(0, GROUP, step, 0)
    total = collect(partial, ATOMS)
    before = [
        piece
        for a in range(GROUP)
        for piece in (sum_ref[a * GROUPS : (a + 1) * GROUPS, :], jnp.zeros((GROUPS, WIDTH), F32))
    ]
    msg = ((total + jnp.concatenate(before, axis=0)) * message_scale).astype(BF)
    row = iota((ATOMS, ATOMS), 0)
    lane = iota((ATOMS, ATOMS), 1)
    row_atom = (row % GROUPS) * GROUP + row // 16
    mine = dot(pick(lane == row_atom), table[...])

    def silu(x):
        h = 0.5 * x
        return h * jnp.tanh(h) + h

    hidden = silu(dot(msg, wm_ref[...])).astype(BF)
    updated = (mine + dot(hidden, wu_ref[...])).astype(BF)
    readout = silu(dot(updated, wr_ref[...])).astype(BF)
    lane_atom = (lane % GROUPS) * GROUP + lane // 16
    out = jnp.zeros((4, ATOMS), F32)
    for f, turn in enumerate((rot, other)):
        back = pick((local(row) == lane_atom) & ((lane // GROUPS) % 2 == f))
        heads = dot_t(wh_ref[...], dot(back, readout).astype(BF))
        force = [
            turn[0][c] * heads[0:1] + turn[1][c] * heads[1:2] + turn[2][c] * heads[2:3] for c in range(3)
        ]
        out = out + jnp.concatenate(force + [heads[3:4]], axis=0)
    out_ref[...] = out


def cost(microseconds):
    return pl.CostEstimate(flops=microseconds * 10**9, bytes_accessed=microseconds * 10**6, transcendentals=0)


def local_step(
    features,
    positions,
    neighbours,
    counts,
    send_rows,
    frames,
    w_edge,
    b_edge,
    w_message,
    w_update,
    w_readout,
    w_heads,
):
    dom_count = lax.axis_size("dom")
    frame_count = lax.axis_size("frame")
    frame = jnp.transpose(frames, (1, 0, 2))
    bias = b_edge.reshape(1, WIDTH)
    inputs = (features, positions, frame, neighbours, counts.reshape(1, ATOMS), w_edge, bias, w_heads.T)
    prepared = [
        pltpu.VMEM((HALF, WIDTH), F32),
        pltpu.VMEM((TABLE, ATOMS), BF),
        pltpu.VMEM((ATOMS, WIDTH), BF),
        pltpu.VMEM((OWN_AT[-1], ATOMS), BF),
        pltpu.VMEM((GROUP, ATOMS, WIDTH), BF),
        pltpu.VMEM((GROUP, ATOMS, ATOMS), BF),
    ]
    payload, *first = pl.pallas_call(
        first_kernel,
        out_shape=[pltpu.VMEM((CAP, PAY), BF)] + [pltpu.VMEM(x.shape, x.dtype) for x in inputs] + prepared,
        scratch_shapes=[pltpu.VMEM((WIDTH // 128, HALF * 8, 128), F32)],
        compiler_params=pltpu.CompilerParams(vmem_limit_bytes=20 << 20),
        cost_estimate=cost(2),
    )(*[pltpu.with_memory_space_constraint(x, pltpu.MemorySpace.HBM) for x in (send_rows, *inputs)])
    held, before = first[:8], first[8:]
    pairs = []
    for d in range(dom_count):
        for f in range(frame_count):
            to = (d + 1) % dom_count if f >= frame_count // 2 else (d - 1) % dom_count
            pairs.append((d * frame_count + f, to * frame_count + (f + frame_count // 2) % frame_count))
    ghosts = lax.ppermute(payload, ("dom", "frame"), pairs)
    own = pl.pallas_call(
        own_kernel,
        out_shape=prepared,
        scratch_shapes=[pltpu.VMEM((WIDTH // 128, HALF * 8, 128), F32)],
        compiler_params=pltpu.CompilerParams(vmem_limit_bytes=20 << 20),
        cost_estimate=cost(5),
    )(*held[:7], *before)
    part = pl.pallas_call(
        last_kernel,
        out_shape=jax.ShapeDtypeStruct((4, ATOMS), F32),
        scratch_shapes=[
            pltpu.VMEM((GHOST_AT[-1], ATOMS), BF),
            pltpu.VMEM((GROUP, ATOMS, WIDTH), BF),
            pltpu.VMEM((GROUP, CAP, ATOMS), BF),
            pltpu.VMEM((WIDTH // 128, ATOMS * 8, 128), F32),
        ],
        compiler_params=pltpu.CompilerParams(vmem_limit_bytes=20 << 20),
        cost_estimate=cost(7),
    )(
        ghosts,
        *own,
        held[1],
        held[2],
        held[5],
        held[6],
        w_message,
        w_update,
        w_readout,
        held[7],
    )
    copies = jnp.broadcast_to(part, (frame_count, *part.shape))
    everything = lax.all_to_all(copies, "frame", split_axis=0, concat_axis=0, tiled=True)
    return jnp.sum(everything, axis=0) / frame_count


def solution(mesh):
    placed = (
        P("dom", None),
        P(None, "dom"),
        P("dom", None),
        P("dom"),
        P("dom", None, None),
        P("frame", None, None),
        P(),
        P(),
        P(),
        P(),
        P(),
        P(),
    )
    return jax.shard_map(
        local_step, mesh=mesh, in_specs=placed, out_specs=P(None, "dom"), check_vma=False
    )
```

```python
import jax
import jax.numpy as jnp
from jax import lax
from jax.experimental import pallas as pl
from jax.experimental.pallas import tpu as pltpu
from jax.sharding import PartitionSpec as P

BF = jnp.bfloat16
F32 = jnp.float32
I32 = jnp.int32
message_scale = 0.0884
radial_step = 1.25

ATOMS = 128
HALF = 64
CAP = 64
TABLE = CAP + ATOMS
WIDTH = 512
SLOTS = 128
FEATS = 16
GROUP = 8
GROUPS = HALF // GROUP
EXTRA = 128
PAY = WIDTH + EXTRA
RADIAL = 6
GHOST_ROWS = ((0, 64), (16, 64), (32, 64), (48, 64))
OWN_ROWS = ((0, 64), (0, 96), (0, 112), (0, 128))
TILE = 256
AHEAD = 4


def iota(shape, dim):
    return lax.broadcasted_iota(I32, shape, dim)


def dot(a, b):
    return jnp.dot(a, b, preferred_element_type=F32)


def dot_t(a, b):
    return lax.dot_general(a, b, (((1,), (1,)), ((), ())), preferred_element_type=F32)


def mask(cond):
    return jnp.where(cond, 1.0, 0.0).astype(F32)


def pick(cond):
    return mask(cond).astype(BF)


def parity():
    return lax.axis_index("frame") // (lax.axis_size("frame") // 2)


def local(n):
    return jnp.where(parity() == 1, ATOMS - 1 - n, n)


def entries(ref):
    return [[ref[a, :, c : c + 1] for c in range(3)] for a in range(3)]


def vectors(rot, we_ref, c):
    return 0.5 * (rot[0][c] * we_ref[6:7, :] + rot[1][c] * we_ref[7:8, :] + rot[2][c] * we_ref[8:9, :])


def split(x):
    high = x.astype(BF).astype(F32)
    return high, x - high


def centres(pos_ref):
    atom = local(iota((8, ATOMS), 1))
    in_group = mask(atom // GROUP == iota((8, ATOMS), 0))
    spread = pick(local(iota((ATOMS, ATOMS), 0)) % GROUP == iota((ATOMS, ATOMS), 1) // FEATS)
    return [dot((in_group * pos_ref[c : c + 1, :].astype(F32)).astype(BF), spread) for c in range(3)]


def placed_rows(chosen, pos_ref):
    ones = jnp.ones((ATOMS, ATOMS), BF)
    return [dot((chosen * pos_ref[c : c + 1, :].astype(F32)).astype(BF), ones) for c in range(3)]


def fill_edges(edges, reach, centre, bounds):
    kind = iota((1, ATOMS), 1) % FEATS
    shift = kind.astype(F32) * radial_step
    at = 0
    for g in range(GROUPS):
        lo, hi = bounds[g // 2]
        rel = [reach[c][lo:hi] - centre[c][g : g + 1, :] for c in range(3)]
        dist = jnp.sqrt(rel[0] * rel[0] + rel[1] * rel[1] + rel[2] * rel[2] + 0.25) - shift
        value = jnp.exp(-(dist * dist))
        axis = jnp.where(kind % 3 == 0, rel[0], jnp.where(kind % 3 == 1, rel[1], rel[2]))
        high, low = split(axis)
        axis = jnp.where((kind >= 9) & (kind < 12), low, high)
        value = jnp.where(kind < RADIAL, value, jnp.where(kind < 15, axis, 1.0))
        edges[at : at + hi - lo, :] = value.astype(BF)
        at += hi - lo


def fill_filter(rhs, rot, we_ref, be_ref):
    vec = jnp.concatenate([vectors(rot, we_ref, c) for c in range(3)], axis=0)
    high, low = split(vec)
    rows = jnp.concatenate([0.5 * we_ref[0:RADIAL, :], high, high, low, 0.5 * be_ref[...]], axis=0)
    rows = jnp.concatenate([rows] * GROUP, axis=0).astype(BF)
    block = iota((ATOMS, WIDTH), 0) // FEATS
    for a in range(GROUP):
        rhs[a, :, :] = jnp.where(block == a, rows, jnp.zeros_like(rows))


def fill_times(times, total):
    for a in range(GROUP):
        spread = pick(iota((ATOMS, ATOMS), 0) % HALF == iota((ATOMS, ATOMS), 1) * GROUP + a)
        times[a, :, :] = dot(total, spread).astype(BF)


def sum_rows(prod, rows):
    parts = [prod[r : r + 16] for r in range(0, rows, 16)]
    while len(parts) > SUMS:
        parts = [
            parts[q] + parts[q + 1] if q + 1 < len(parts) else parts[q] for q in range(0, len(parts), 2)
        ]
    total = parts[0].astype(F32)
    for part in parts[1:]:
        total = total + part.astype(F32)
    return total[:8] + total[8:]


SUMS = 1


def offsets_of(bounds):
    offsets = [0]
    for g in range(GROUPS):
        lo, hi = bounds[g // 2]
        offsets.append(offsets[-1] + hi - lo)
    return offsets


OWN_AT = offsets_of(OWN_ROWS)
GHOST_AT = offsets_of(GHOST_ROWS)


def gated(pre):
    half = pre.astype(BF)
    return half * jnp.tanh(half) + half


def cut(rows):
    return [rows[r : r + 16] for r in range(0, rows.shape[0], 16)]


def total_of(parts):
    while len(parts) > SUMS:
        parts = [
            parts[q] + parts[q + 1] if q + 1 < len(parts) else parts[q] for q in range(0, len(parts), 2)
        ]
    total = parts[0].astype(F32)
    for part in parts[1:]:
        total = total + part.astype(F32)
    return total[:8] + total[8:]


def keep(partial, a, k, count, w, done):
    at = pl.multiple_of((a * count + k) * 8, 8)
    for t in range(TILE // 128):
        partial[w * (TILE // 128) + t, pl.ds(at, 8), :] = done[:, t * 128 : (t + 1) * 128]


def collect(partial, begin, end):
    tiles = []
    for t in range(WIDTH // 128):
        total = partial[t, pl.ds(begin * 8, end - begin, stride=8), :]
        for r in range(1, 8):
            total = total + partial[t, pl.ds(begin * 8 + r, end - begin, stride=8), :]
        tiles.append(total)
    return jnp.concatenate(tiles, axis=1)


def early():
    return (lax.axis_index("dom") == 0) & (parity() == 0)


def sum_own(begin, end, table, edges, rhs, times, partial, sum_ref):
    def step(a, carry):
        share = times[a]
        for w in range(WIDTH // TILE):
            span = slice(w * TILE, (w + 1) * TILE)
            for first in range(0, GROUPS, 2):
                pre = dot(edges[OWN_AT[first] : OWN_AT[first + 2], :], rhs[a, :, span]).astype(BF)
                for g in range(first, first + 2):
                    lo, hi = OWN_ROWS[g // 2]
                    weighted = table[lo:hi, span] * share[lo:hi, g : g + 1]
                    gate = gated(pre[OWN_AT[g] - OWN_AT[first] : OWN_AT[g + 1] - OWN_AT[first]])
                    keep(partial, a, g, GROUPS, w, total_of(cut(gate * weighted)))
        return carry

    lax.fori_loop(begin, end, step, 0)
    sum_ref[begin * GROUPS : end * GROUPS, :] = collect(partial, begin * GROUPS, end * GROUPS)


def prepare_and_sum(
    end,
    feat_ref,
    pos_ref,
    frame_ref,
    nbr_ref,
    cnt_ref,
    we_ref,
    be_ref,
    sum_ref,
    total_ref,
    table,
    edges,
    rhs,
    times,
    partial,
):
    own = pick(iota((ATOMS, ATOMS), 1) == local(iota((ATOMS, ATOMS), 0)))
    table[...] = dot(own, feat_ref[...]).astype(BF)

    raw = nbr_ref[...]
    order = jnp.where(raw < ATOMS, raw + CAP, jnp.where(raw < ATOMS + CAP, raw - ATOMS, raw))
    order = jnp.where(parity() == 1, 2 * CAP + ATOMS - 1 - order, order)
    by_slot = order.astype(F32).T.astype(BF)
    atom = local(iota((ATOMS, ATOMS), 0))
    lane = iota((ATOMS, ATOMS), 1)
    to_low = pick((atom == lane) & (lane < HALF))
    to_high = pick(atom + HALF == lane)
    folded = dot(by_slot[: SLOTS // 2], to_low) + dot(by_slot[SLOTS // 2 :], to_high)
    cnt = jnp.broadcast_to(cnt_ref[...].astype(F32), (8, ATOMS)).astype(BF)
    live = (dot(cnt, to_low) + dot(cnt, to_high))[0:1, :]
    slot = iota((SLOTS // 2, ATOMS), 0) + jnp.where(iota((SLOTS // 2, ATOMS), 1) < HALF, 0, SLOTS // 2)
    folded = jnp.where(slot.astype(F32) < live, folded, -1.0).astype(BF)
    place = iota((TABLE, ATOMS), 0).astype(F32).astype(BF)
    total = jnp.zeros((TABLE, ATOMS), BF)
    one = jnp.ones((TABLE, ATOMS), BF)
    for k in range(SLOTS // 2):
        total = jnp.where(place == folded[k : k + 1, :], total + one, total)
    total_ref[...] = total
    fill_times(times, total[CAP:])
    fill_edges(edges, placed_rows(own.astype(F32), pos_ref), centres(pos_ref), OWN_ROWS)
    fill_filter(rhs, entries(frame_ref), we_ref, be_ref)
    sum_own(0, end, table, edges, rhs, times, partial, sum_ref)


def first_kernel(rows_ref, *refs):
    sources, (pay_ref,), results, partial = refs[:8], refs[8:9], refs[9:23], refs[23]
    for source, result in zip(sources, results[:8]):
        result[...] = source[...]
    feat_ref, pos_ref, frame_ref = sources[:3]
    wanted = jnp.where(parity() == 1, rows_ref[0, 1:2, :], rows_ref[0, 0:1, :])
    row = iota((CAP, CAP), 0)
    source = jnp.where(parity() == 1, row, CAP - 1 - row)
    column = jnp.sum(
        jnp.where(iota((CAP, CAP), 1) == source, wanted, 0).astype(F32), axis=1, keepdims=True
    ).astype(I32)
    chosen = pick(iota((CAP, ATOMS), 1) == column)
    pay_ref[:, :WIDTH] = dot(chosen, feat_ref[...]).astype(BF)
    lane = iota((CAP, EXTRA), 1)
    rest = jnp.zeros((CAP, EXTRA), F32)
    for c in range(3):
        line = chosen.astype(F32) * pos_ref[c : c + 1, :].astype(F32)
        rest = jnp.where(lane == c, jnp.sum(line, axis=1, keepdims=True), rest)
    turn = jnp.zeros((CAP, EXTRA), F32)
    for a in range(3):
        for c in range(3):
            k = 8 + 3 * a + c
            here = (lane == k) | (lane == k + 16) | (lane == k + 32)
            turn = jnp.where(here, frame_ref[a, :, c : c + 1], turn)
    high, rest_of = split(turn)
    mid, low = split(rest_of)
    turn = jnp.where(lane < 24, high, jnp.where(lane < 40, mid, low))
    pay_ref[:, WIDTH:] = (rest + turn).astype(BF)

    @pl.when(early())
    def _():
        prepare_and_sum(AHEAD, *sources[:7], *results[8:], partial)


def own_kernel(*refs):
    sources, before, results, partial = refs[:7], refs[7:13], refs[13:19], refs[19]

    @pl.when(early())
    def _():
        for source, result in zip(before, results):
            result[...] = source[...]
        sum_own(AHEAD, GROUP, *results[2:], partial, results[0])

    @pl.when(jnp.logical_not(early()))
    def _():
        prepare_and_sum(GROUP, *sources, *results, partial)


def last_kernel(
    pay_ref,
    sum_ref,
    total_ref,
    table,
    edges,
    rhs,
    own_times,
    pos_ref,
    frame_ref,
    we_ref,
    be_ref,
    wm_ref,
    wu_ref,
    wr_ref,
    wh_ref,
    out_ref,
    ghosts,
    rhs_other,
    times,
    partial,
):
    rot = entries(frame_ref)
    extra = pay_ref[:, WIDTH:]
    head = extra[0:1, :].astype(F32)
    other = []
    for a in range(3):
        other.append([])
        for c in range(3):
            k = 8 + 3 * a + c
            other[a].append(head[:, k : k + 1] + head[:, k + 16 : k + 17] + head[:, k + 32 : k + 33])
    reach = [dot(extra, pick(iota((EXTRA, EXTRA), 0) == c)) for c in range(3)]
    fill_times(times, total_ref[:CAP, :])
    fill_edges(ghosts, reach, centres(pos_ref), GHOST_ROWS)
    fill_filter(rhs_other, other, we_ref, be_ref)

    def step(a, carry):
        share = times[a]
        own_share = own_times[a]
        for w in range(WIDTH // TILE):
            span = slice(w * TILE, (w + 1) * TILE)
            near = gated(dot(ghosts[...], rhs[a, :, span]))
            far = gated(dot(ghosts[...], rhs_other[a, :, span]))
            for first in range(0, GROUPS, 2):
                pre = dot(edges[OWN_AT[first] : OWN_AT[first + 2], :], rhs_other[a, :, span]).astype(BF)
                for g in range(first, first + 2):
                    lo, hi = GHOST_ROWS[g // 2]
                    weighted = pay_ref[lo:hi, span] * share[lo:hi, g : g + 1]
                    rows = slice(GHOST_AT[g], GHOST_AT[g + 1])
                    keep(partial, a, g, 2 * GROUPS, w, total_of(cut(near[rows] * weighted)))
                    parts = cut(far[rows] * weighted)
                    lo, hi = OWN_ROWS[g // 2]
                    weighted = table[lo:hi, span] * own_share[lo:hi, g : g + 1]
                    gate = gated(pre[OWN_AT[g] - OWN_AT[first] : OWN_AT[g + 1] - OWN_AT[first]])
                    parts = parts + cut(gate * weighted)
                    keep(partial, a, GROUPS + g, 2 * GROUPS, w, total_of(parts))
        return carry

    lax.fori_loop(0, GROUP, step, 0)
    total = collect(partial, 0, ATOMS)
    before = [
        piece
        for a in range(GROUP)
        for piece in (sum_ref[a * GROUPS : (a + 1) * GROUPS, :], jnp.zeros((GROUPS, WIDTH), F32))
    ]
    msg = ((total + jnp.concatenate(before, axis=0)) * message_scale).astype(BF)
    row = iota((ATOMS, ATOMS), 0)
    lane = iota((ATOMS, ATOMS), 1)
    row_atom = (row % GROUPS) * GROUP + row // 16
    mine = dot(pick(lane == row_atom), table[...])

    def silu(x):
        h = 0.5 * x
        return h * jnp.tanh(h) + h

    hidden = silu(dot(msg, wm_ref[...])).astype(BF)
    updated = (mine + dot(hidden, wu_ref[...])).astype(BF)
    readout = silu(dot(updated, wr_ref[...])).astype(BF)
    lane_atom = (lane % GROUPS) * GROUP + lane // 16
    out = jnp.zeros((4, ATOMS), F32)
    for f, turn in enumerate((rot, other)):
        back = pick((local(row) == lane_atom) & ((lane // GROUPS) % 2 == f))
        heads = dot_t(wh_ref[...], dot(back, readout).astype(BF))
        force = [
            turn[0][c] * heads[0:1] + turn[1][c] * heads[1:2] + turn[2][c] * heads[2:3] for c in range(3)
        ]
        out = out + jnp.concatenate(force + [heads[3:4]], axis=0)
    out_ref[...] = out


def cost(microseconds):
    return pl.CostEstimate(flops=microseconds * 10**9, bytes_accessed=microseconds * 10**6, transcendentals=0)


def local_step(
    features,
    positions,
    neighbours,
    counts,
    send_rows,
    frames,
    w_edge,
    b_edge,
    w_message,
    w_update,
    w_readout,
    w_heads,
):
    dom_count = lax.axis_size("dom")
    frame_count = lax.axis_size("frame")
    frame = jnp.transpose(frames, (1, 0, 2))
    bias = b_edge.reshape(1, WIDTH)
    inputs = (features, positions, frame, neighbours, counts.reshape(1, ATOMS), w_edge, bias, w_heads.T)
    prepared = [
        pltpu.VMEM((HALF, WIDTH), F32),
        pltpu.VMEM((TABLE, ATOMS), BF),
        pltpu.VMEM((ATOMS, WIDTH), BF),
        pltpu.VMEM((OWN_AT[-1], ATOMS), BF),
        pltpu.VMEM((GROUP, ATOMS, WIDTH), BF),
        pltpu.VMEM((GROUP, ATOMS, ATOMS), BF),
    ]
    payload, *first = pl.pallas_call(
        first_kernel,
        out_shape=[pltpu.VMEM((CAP, PAY), BF)] + [pltpu.VMEM(x.shape, x.dtype) for x in inputs] + prepared,
        scratch_shapes=[pltpu.VMEM((WIDTH // 128, HALF * 8, 128), F32)],
        compiler_params=pltpu.CompilerParams(vmem_limit_bytes=20 << 20),
        cost_estimate=cost(2),
    )(*[pltpu.with_memory_space_constraint(x, pltpu.MemorySpace.HBM) for x in (send_rows, *inputs)])
    held, before = first[:8], first[8:]
    pairs = []
    for d in range(dom_count):
        for f in range(frame_count):
            to = (d + 1) % dom_count if f >= frame_count // 2 else (d - 1) % dom_count
            pairs.append((d * frame_count + f, to * frame_count + (f + frame_count // 2) % frame_count))
    ghosts = lax.ppermute(payload, ("dom", "frame"), pairs)
    own = pl.pallas_call(
        own_kernel,
        out_shape=prepared,
        scratch_shapes=[pltpu.VMEM((WIDTH // 128, HALF * 8, 128), F32)],
        compiler_params=pltpu.CompilerParams(vmem_limit_bytes=20 << 20),
        cost_estimate=cost(5),
    )(*held[:7], *before)
    part = pl.pallas_call(
        last_kernel,
        out_shape=jax.ShapeDtypeStruct((4, ATOMS), F32),
        scratch_shapes=[
            pltpu.VMEM((GHOST_AT[-1], ATOMS), BF),
            pltpu.VMEM((GROUP, ATOMS, WIDTH), BF),
            pltpu.VMEM((GROUP, CAP, ATOMS), BF),
            pltpu.VMEM((WIDTH // 128, ATOMS * 8, 128), F32),
        ],
        compiler_params=pltpu.CompilerParams(vmem_limit_bytes=20 << 20),
        cost_estimate=cost(7),
    )(
        ghosts,
        *own,
        held[1],
        held[2],
        held[5],
        held[6],
        w_message,
        w_update,
        w_readout,
        held[7],
    )
    copies = jnp.broadcast_to(part, (frame_count, *part.shape))
    everything = lax.all_to_all(copies, "frame", split_axis=0, concat_axis=0, tiled=True)
    return jnp.sum(everything, axis=0) / frame_count


def solution(mesh):
    placed = (
        P("dom", None),
        P(None, "dom"),
        P("dom", None),
        P("dom"),
        P("dom", None, None),
        P("frame", None, None),
        P(),
        P(),
        P(),
        P(),
        P(),
        P(),
    )
    return jax.shard_map(
        local_step, mesh=mesh, in_specs=placed, out_specs=P(None, "dom"), check_vma=False
    )
```

```python
import jax
import jax.numpy as jnp
from jax import lax
from jax.experimental import pallas as pl
from jax.experimental.pallas import tpu as pltpu
from jax.sharding import PartitionSpec as P

BF = jnp.bfloat16
F32 = jnp.float32
I32 = jnp.int32
message_scale = 0.0884
radial_step = 1.25

ATOMS = 128
HALF = 64
CAP = 64
TABLE = CAP + ATOMS
WIDTH = 512
SLOTS = 128
FEATS = 16
GROUP = 8
GROUPS = HALF // GROUP
EXTRA = 128
PAY = WIDTH + EXTRA
RADIAL = 6
GHOST_ROWS = ((0, 64), (16, 64), (32, 64), (48, 64))
OWN_ROWS = ((0, 64), (0, 96), (0, 112), (0, 128))
TILE = 256
AHEAD = 4


def iota(shape, dim):
    return lax.broadcasted_iota(I32, shape, dim)


def dot(a, b):
    return jnp.dot(a, b, preferred_element_type=F32)


def dot_t(a, b):
    return lax.dot_general(a, b, (((1,), (1,)), ((), ())), preferred_element_type=F32)


def mask(cond):
    return jnp.where(cond, 1.0, 0.0).astype(F32)


def pick(cond):
    return mask(cond).astype(BF)


def parity():
    return lax.axis_index("frame") // (lax.axis_size("frame") // 2)


def local(n):
    return jnp.where(parity() == 1, ATOMS - 1 - n, n)


def entries(ref):
    return [[ref[a, :, c : c + 1] for c in range(3)] for a in range(3)]


def vectors(rot, we_ref, c):
    return 0.5 * (rot[0][c] * we_ref[6:7, :] + rot[1][c] * we_ref[7:8, :] + rot[2][c] * we_ref[8:9, :])


def split(x):
    high = x.astype(BF).astype(F32)
    return high, x - high


def centres(pos_ref):
    atom = local(iota((8, ATOMS), 1))
    in_group = mask(atom // GROUP == iota((8, ATOMS), 0))
    spread = pick(local(iota((ATOMS, ATOMS), 0)) % GROUP == iota((ATOMS, ATOMS), 1) // FEATS)
    return [dot((in_group * pos_ref[c : c + 1, :].astype(F32)).astype(BF), spread) for c in range(3)]


def placed_rows(chosen, pos_ref):
    ones = jnp.ones((ATOMS, ATOMS), BF)
    return [dot((chosen * pos_ref[c : c + 1, :].astype(F32)).astype(BF), ones) for c in range(3)]


def fill_edges(edges, reach, centre, bounds):
    kind = iota((1, ATOMS), 1) % FEATS
    shift = kind.astype(F32) * radial_step
    at = 0
    for g in range(GROUPS):
        lo, hi = bounds[g // 2]
        rel = [reach[c][lo:hi] - centre[c][g : g + 1, :] for c in range(3)]
        dist = jnp.sqrt(rel[0] * rel[0] + rel[1] * rel[1] + rel[2] * rel[2] + 0.25) - shift
        value = jnp.exp(-(dist * dist))
        axis = jnp.where(kind % 3 == 0, rel[0], jnp.where(kind % 3 == 1, rel[1], rel[2]))
        high, low = split(axis)
        axis = jnp.where((kind >= 9) & (kind < 12), low, high)
        value = jnp.where(kind < RADIAL, value, jnp.where(kind < 15, axis, 1.0))
        edges[at : at + hi - lo, :] = value.astype(BF)
        at += hi - lo


def fill_filter(rhs, rot, we_ref, be_ref):
    vec = jnp.concatenate([vectors(rot, we_ref, c) for c in range(3)], axis=0)
    high, low = split(vec)
    rows = jnp.concatenate([0.5 * we_ref[0:RADIAL, :], high, high, low, 0.5 * be_ref[...]], axis=0)
    room = ATOMS - FEATS
    rhs[:room, :] = jnp.zeros((room, WIDTH), BF)
    rhs[room : room + FEATS, :] = rows.astype(BF)
    rhs[room + FEATS :, :] = jnp.zeros((room, WIDTH), BF)


def weights_at(rhs, a, span):
    first = (GROUP - 1 - a) * FEATS
    return rhs[first : first + ATOMS, span]


def fill_times(times, total):
    for a in range(GROUP):
        spread = pick(iota((ATOMS, ATOMS), 0) % HALF == iota((ATOMS, ATOMS), 1) * GROUP + a)
        times[a, :, :] = dot(total, spread).astype(BF)


def sum_rows(prod, rows):
    parts = [prod[r : r + 16] for r in range(0, rows, 16)]
    while len(parts) > SUMS:
        parts = [
            parts[q] + parts[q + 1] if q + 1 < len(parts) else parts[q] for q in range(0, len(parts), 2)
        ]
    total = parts[0].astype(F32)
    for part in parts[1:]:
        total = total + part.astype(F32)
    return total[:8] + total[8:]


SUMS = 1


def offsets_of(bounds):
    offsets = [0]
    for g in range(GROUPS):
        lo, hi = bounds[g // 2]
        offsets.append(offsets[-1] + hi - lo)
    return offsets


OWN_AT = offsets_of(OWN_ROWS)
GHOST_AT = offsets_of(GHOST_ROWS)


def gated(pre):
    half = pre.astype(BF)
    return half * jnp.tanh(half) + half


def cut(rows):
    return [rows[r : r + 16] for r in range(0, rows.shape[0], 16)]


def total_of(parts):
    while len(parts) > SUMS:
        parts = [
            parts[q] + parts[q + 1] if q + 1 < len(parts) else parts[q] for q in range(0, len(parts), 2)
        ]
    total = parts[0].astype(F32)
    for part in parts[1:]:
        total = total + part.astype(F32)
    return total[:8] + total[8:]


def keep(partial, a, k, count, w, done):
    at = (a * count + k) * 8
    for t in range(TILE // 128):
        partial[w * (TILE // 128) + t, at : at + 8, :] = done[:, t * 128 : (t + 1) * 128]


def collect(partial, begin, end):
    tiles = []
    for t in range(WIDTH // 128):
        total = partial[t, pl.ds(begin * 8, end - begin, stride=8), :]
        for r in range(1, 8):
            total = total + partial[t, pl.ds(begin * 8 + r, end - begin, stride=8), :]
        tiles.append(total)
    return jnp.concatenate(tiles, axis=1)


def early():
    return (lax.axis_index("dom") == 0) & (parity() == 0)


def sum_own(begin, end, table, edges, rhs, times, partial, sum_ref):
    def step(a):
        share = times[a]
        for w in range(WIDTH // TILE):
            span = slice(w * TILE, (w + 1) * TILE)
            for first in range(0, GROUPS, 2):
                pre = dot(edges[OWN_AT[first] : OWN_AT[first + 2], :], weights_at(rhs, a, span)).astype(BF)
                for g in range(first, first + 2):
                    lo, hi = OWN_ROWS[g // 2]
                    weighted = table[lo:hi, span] * share[lo:hi, g : g + 1]
                    gate = gated(pre[OWN_AT[g] - OWN_AT[first] : OWN_AT[g + 1] - OWN_AT[first]])
                    keep(partial, a, g, GROUPS, w, total_of(cut(gate * weighted)))

    for a in range(begin, end):
        step(a)
    sum_ref[begin * GROUPS : end * GROUPS, :] = collect(partial, begin * GROUPS, end * GROUPS)


def prepare_and_sum(
    end,
    feat_ref,
    pos_ref,
    frame_ref,
    nbr_ref,
    cnt_ref,
    we_ref,
    be_ref,
    sum_ref,
    total_ref,
    table,
    edges,
    rhs,
    times,
    partial,
):
    own = pick(iota((ATOMS, ATOMS), 1) == local(iota((ATOMS, ATOMS), 0)))
    table[...] = dot(own, feat_ref[...]).astype(BF)

    raw = nbr_ref[...]
    order = jnp.where(raw < ATOMS, raw + CAP, jnp.where(raw < ATOMS + CAP, raw - ATOMS, raw))
    order = jnp.where(parity() == 1, 2 * CAP + ATOMS - 1 - order, order)
    by_slot = order.astype(F32).T.astype(BF)
    atom = local(iota((ATOMS, ATOMS), 0))
    lane = iota((ATOMS, ATOMS), 1)
    to_low = pick((atom == lane) & (lane < HALF))
    to_high = pick(atom + HALF == lane)
    folded = dot(by_slot[: SLOTS // 2], to_low) + dot(by_slot[SLOTS // 2 :], to_high)
    cnt = jnp.broadcast_to(cnt_ref[...].astype(F32), (8, ATOMS)).astype(BF)
    live = (dot(cnt, to_low) + dot(cnt, to_high))[0:1, :]
    slot = iota((SLOTS // 2, ATOMS), 0) + jnp.where(iota((SLOTS // 2, ATOMS), 1) < HALF, 0, SLOTS // 2)
    folded = jnp.where(slot.astype(F32) < live, folded, -1.0).astype(BF)
    place = iota((TABLE, ATOMS), 0).astype(F32).astype(BF)
    total = jnp.zeros((TABLE, ATOMS), BF)
    one = jnp.ones((TABLE, ATOMS), BF)
    for k in range(SLOTS // 2):
        total = jnp.where(place == folded[k : k + 1, :], total + one, total)
    total_ref[...] = total
    fill_times(times, total[CAP:])
    fill_edges(edges, placed_rows(own.astype(F32), pos_ref), centres(pos_ref), OWN_ROWS)
    fill_filter(rhs, entries(frame_ref), we_ref, be_ref)
    sum_own(0, end, table, edges, rhs, times, partial, sum_ref)


def first_kernel(rows_ref, *refs):
    sources, (pay_ref,), results, partial = refs[:8], refs[8:9], refs[9:23], refs[23]
    for source, result in zip(sources, results[:8]):
        result[...] = source[...]
    feat_ref, pos_ref, frame_ref = sources[:3]
    wanted = jnp.where(parity() == 1, rows_ref[0, 1:2, :], rows_ref[0, 0:1, :])
    row = iota((CAP, CAP), 0)
    source = jnp.where(parity() == 1, row, CAP - 1 - row)
    column = jnp.sum(
        jnp.where(iota((CAP, CAP), 1) == source, wanted, 0).astype(F32), axis=1, keepdims=True
    ).astype(I32)
    chosen = pick(iota((CAP, ATOMS), 1) == column)
    pay_ref[:, :WIDTH] = dot(chosen, feat_ref[...]).astype(BF)
    lane = iota((CAP, EXTRA), 1)
    rest = jnp.zeros((CAP, EXTRA), F32)
    for c in range(3):
        line = chosen.astype(F32) * pos_ref[c : c + 1, :].astype(F32)
        rest = jnp.where(lane == c, jnp.sum(line, axis=1, keepdims=True), rest)
    turn = jnp.zeros((CAP, EXTRA), F32)
    for a in range(3):
        for c in range(3):
            k = 8 + 3 * a + c
            here = (lane == k) | (lane == k + 16) | (lane == k + 32)
            turn = jnp.where(here, frame_ref[a, :, c : c + 1], turn)
    high, rest_of = split(turn)
    mid, low = split(rest_of)
    turn = jnp.where(lane < 24, high, jnp.where(lane < 40, mid, low))
    pay_ref[:, WIDTH:] = (rest + turn).astype(BF)

    @pl.when(early())
    def _():
        prepare_and_sum(AHEAD, *sources[:7], *results[8:], partial)


def own_kernel(*refs):
    sources, before, results, partial = refs[:7], refs[7:13], refs[13:19], refs[19]

    @pl.when(early())
    def _():
        for source, result in zip(before, results):
            result[...] = source[...]
        sum_own(AHEAD, GROUP, *results[2:], partial, results[0])

    @pl.when(jnp.logical_not(early()))
    def _():
        prepare_and_sum(GROUP, *sources, *results, partial)


def last_kernel(
    pay_ref,
    sum_ref,
    total_ref,
    table,
    edges,
    rhs,
    own_times,
    pos_ref,
    frame_ref,
    we_ref,
    be_ref,
    wm_ref,
    wu_ref,
    wr_ref,
    wh_ref,
    out_ref,
    ghosts,
    rhs_other,
    times,
    partial,
):
    rot = entries(frame_ref)
    extra = pay_ref[:, WIDTH:]
    head = extra[0:1, :].astype(F32)
    other = []
    for a in range(3):
        other.append([])
        for c in range(3):
            k = 8 + 3 * a + c
            other[a].append(head[:, k : k + 1] + head[:, k + 16 : k + 17] + head[:, k + 32 : k + 33])
    reach = [dot(extra, pick(iota((EXTRA, EXTRA), 0) == c)) for c in range(3)]
    fill_times(times, total_ref[:CAP, :])
    fill_edges(ghosts, reach, centres(pos_ref), GHOST_ROWS)
    fill_filter(rhs_other, other, we_ref, be_ref)

    def step(a):
        share = times[a]
        own_share = own_times[a]
        for w in range(WIDTH // TILE):
            span = slice(w * TILE, (w + 1) * TILE)
            near = gated(dot(ghosts[...], weights_at(rhs, a, span)))
            far = gated(dot(ghosts[...], weights_at(rhs_other, a, span)))
            for first in range(0, GROUPS, 2):
                pre = dot(edges[OWN_AT[first] : OWN_AT[first + 2], :], weights_at(rhs_other, a, span)).astype(BF)
                for g in range(first, first + 2):
                    lo, hi = GHOST_ROWS[g // 2]
                    weighted = pay_ref[lo:hi, span] * share[lo:hi, g : g + 1]
                    rows = slice(GHOST_AT[g], GHOST_AT[g + 1])
                    keep(partial, a, g, 2 * GROUPS, w, total_of(cut(near[rows] * weighted)))
                    parts = cut(far[rows] * weighted)
                    lo, hi = OWN_ROWS[g // 2]
                    weighted = table[lo:hi, span] * own_share[lo:hi, g : g + 1]
                    gate = gated(pre[OWN_AT[g] - OWN_AT[first] : OWN_AT[g + 1] - OWN_AT[first]])
                    parts = parts + cut(gate * weighted)
                    keep(partial, a, GROUPS + g, 2 * GROUPS, w, total_of(parts))

    for a in range(GROUP):
        step(a)
    total = collect(partial, 0, ATOMS)
    before = [
        piece
        for a in range(GROUP)
        for piece in (sum_ref[a * GROUPS : (a + 1) * GROUPS, :], jnp.zeros((GROUPS, WIDTH), F32))
    ]
    msg = ((total + jnp.concatenate(before, axis=0)) * message_scale).astype(BF)
    row = iota((ATOMS, ATOMS), 0)
    lane = iota((ATOMS, ATOMS), 1)
    row_atom = (row % GROUPS) * GROUP + row // 16
    mine = dot(pick(lane == row_atom), table[...])

    def silu(x):
        h = 0.5 * x
        return h * jnp.tanh(h) + h

    hidden = silu(dot(msg, wm_ref[...])).astype(BF)
    updated = (mine + dot(hidden, wu_ref[...])).astype(BF)
    readout = silu(dot(updated, wr_ref[...])).astype(BF)
    lane_atom = (lane % GROUPS) * GROUP + lane // 16
    out = jnp.zeros((4, ATOMS), F32)
    for f, turn in enumerate((rot, other)):
        back = pick((local(row) == lane_atom) & ((lane // GROUPS) % 2 == f))
        heads = dot_t(wh_ref[...], dot(back, readout).astype(BF))
        force = [
            turn[0][c] * heads[0:1] + turn[1][c] * heads[1:2] + turn[2][c] * heads[2:3] for c in range(3)
        ]
        out = out + jnp.concatenate(force + [heads[3:4]], axis=0)
    out_ref[...] = out


def cost(microseconds):
    return pl.CostEstimate(flops=microseconds * 10**9, bytes_accessed=microseconds * 10**6, transcendentals=0)


def local_step(
    features,
    positions,
    neighbours,
    counts,
    send_rows,
    frames,
    w_edge,
    b_edge,
    w_message,
    w_update,
    w_readout,
    w_heads,
):
    dom_count = lax.axis_size("dom")
    frame_count = lax.axis_size("frame")
    frame = jnp.transpose(frames, (1, 0, 2))
    bias = b_edge.reshape(1, WIDTH)
    inputs = (features, positions, frame, neighbours, counts.reshape(1, ATOMS), w_edge, bias, w_heads.T)
    prepared = [
        pltpu.VMEM((HALF, WIDTH), F32),
        pltpu.VMEM((TABLE, ATOMS), BF),
        pltpu.VMEM((ATOMS, WIDTH), BF),
        pltpu.VMEM((OWN_AT[-1], ATOMS), BF),
        pltpu.VMEM((2 * ATOMS - FEATS, WIDTH), BF),
        pltpu.VMEM((GROUP, ATOMS, ATOMS), BF),
    ]
    payload, *first = pl.pallas_call(
        first_kernel,
        out_shape=[pltpu.VMEM((CAP, PAY), BF)] + [pltpu.VMEM(x.shape, x.dtype) for x in inputs] + prepared,
        scratch_shapes=[pltpu.VMEM((WIDTH // 128, HALF * 8, 128), F32)],
        compiler_params=pltpu.CompilerParams(vmem_limit_bytes=20 << 20),
        cost_estimate=cost(2),
    )(*[pltpu.with_memory_space_constraint(x, pltpu.MemorySpace.HBM) for x in (send_rows, *inputs)])
    held, before = first[:8], first[8:]
    pairs = []
    for d in range(dom_count):
        for f in range(frame_count):
            to = (d + 1) % dom_count if f >= frame_count // 2 else (d - 1) % dom_count
            pairs.append((d * frame_count + f, to * frame_count + (f + frame_count // 2) % frame_count))
    ghosts = lax.ppermute(payload, ("dom", "frame"), pairs)
    own = pl.pallas_call(
        own_kernel,
        out_shape=prepared,
        scratch_shapes=[pltpu.VMEM((WIDTH // 128, HALF * 8, 128), F32)],
        compiler_params=pltpu.CompilerParams(vmem_limit_bytes=20 << 20),
        cost_estimate=cost(5),
    )(*held[:7], *before)
    part = pl.pallas_call(
        last_kernel,
        out_shape=jax.ShapeDtypeStruct((4, ATOMS), F32),
        scratch_shapes=[
            pltpu.VMEM((GHOST_AT[-1], ATOMS), BF),
            pltpu.VMEM((2 * ATOMS - FEATS, WIDTH), BF),
            pltpu.VMEM((GROUP, CAP, ATOMS), BF),
            pltpu.VMEM((WIDTH // 128, ATOMS * 8, 128), F32),
        ],
        compiler_params=pltpu.CompilerParams(vmem_limit_bytes=20 << 20),
        cost_estimate=cost(7),
    )(
        ghosts,
        *own,
        held[1],
        held[2],
        held[5],
        held[6],
        w_message,
        w_update,
        w_readout,
        held[7],
    )
    copies = jnp.broadcast_to(part, (frame_count, *part.shape))
    everything = lax.all_to_all(copies, "frame", split_axis=0, concat_axis=0, tiled=True)
    return jnp.sum(everything, axis=0) / frame_count


def solution(mesh):
    placed = (
        P("dom", None),
        P(None, "dom"),
        P("dom", None),
        P("dom"),
        P("dom", None, None),
        P("frame", None, None),
        P(),
        P(),
        P(),
        P(),
        P(),
        P(),
    )
    return jax.shard_map(
        local_step, mesh=mesh, in_specs=placed, out_specs=P(None, "dom"), check_vma=False
    )
```

```python
import jax
import jax.numpy as jnp
from jax import lax
from jax.experimental import pallas as pl
from jax.experimental.pallas import tpu as pltpu
from jax.sharding import PartitionSpec as P

BF = jnp.bfloat16
F32 = jnp.float32
I32 = jnp.int32
message_scale = 0.0884
radial_step = 1.25

ATOMS = 128
HALF = 64
CAP = 64
TABLE = CAP + ATOMS
WIDTH = 512
SLOTS = 128
FEATS = 16
GROUP = 8
GROUPS = HALF // GROUP
EXTRA = 128
PAY = WIDTH + EXTRA
RADIAL = 6
GHOST_ROWS = ((0, 64), (16, 64), (32, 64), (48, 64))
OWN_ROWS = ((0, 64), (0, 96), (0, 112), (0, 128))
TILE = 256
AHEAD = 3


def iota(shape, dim):
    return lax.broadcasted_iota(I32, shape, dim)


def dot(a, b):
    return jnp.dot(a, b, preferred_element_type=F32)


def dot_t(a, b):
    return lax.dot_general(a, b, (((1,), (1,)), ((), ())), preferred_element_type=F32)


def mask(cond):
    return jnp.where(cond, 1.0, 0.0).astype(F32)


def pick(cond):
    return mask(cond).astype(BF)


def parity():
    return lax.axis_index("frame") // (lax.axis_size("frame") // 2)


def local(n):
    return jnp.where(parity() == 1, ATOMS - 1 - n, n)


def entries(ref):
    return [[ref[a, :, c : c + 1] for c in range(3)] for a in range(3)]


def vectors(rot, we_ref, c):
    return 0.5 * (rot[0][c] * we_ref[6:7, :] + rot[1][c] * we_ref[7:8, :] + rot[2][c] * we_ref[8:9, :])


def split(x):
    high = x.astype(BF).astype(F32)
    return high, x - high


def centres(pos_ref):
    atom = local(iota((8, ATOMS), 1))
    in_group = mask(atom // GROUP == iota((8, ATOMS), 0))
    spread = pick(local(iota((ATOMS, ATOMS), 0)) % GROUP == iota((ATOMS, ATOMS), 1) // FEATS)
    return [dot((in_group * pos_ref[c : c + 1, :].astype(F32)).astype(BF), spread) for c in range(3)]


def placed_rows(chosen, pos_ref):
    ones = jnp.ones((ATOMS, ATOMS), BF)
    return [dot((chosen * pos_ref[c : c + 1, :].astype(F32)).astype(BF), ones) for c in range(3)]


def fill_edges(edges, reach, centre, bounds):
    kind = iota((1, ATOMS), 1) % FEATS
    shift = kind.astype(F32) * radial_step
    at = 0
    for g in range(GROUPS):
        lo, hi = bounds[g // 2]
        rel = [reach[c][lo:hi] - centre[c][g : g + 1, :] for c in range(3)]
        dist = jnp.sqrt(rel[0] * rel[0] + rel[1] * rel[1] + rel[2] * rel[2] + 0.25) - shift
        value = jnp.exp(-(dist * dist))
        axis = jnp.where(kind % 3 == 0, rel[0], jnp.where(kind % 3 == 1, rel[1], rel[2]))
        high, low = split(axis)
        axis = jnp.where((kind >= 9) & (kind < 12), low, high)
        value = jnp.where(kind < RADIAL, value, jnp.where(kind < 15, axis, 1.0))
        edges[at : at + hi - lo, :] = value.astype(BF)
        at += hi - lo


def fill_filter(rhs, rot, we_ref, be_ref):
    vec = jnp.concatenate([vectors(rot, we_ref, c) for c in range(3)], axis=0)
    high, low = split(vec)
    rows = jnp.concatenate([0.5 * we_ref[0:RADIAL, :], high, high, low, 0.5 * be_ref[...]], axis=0)
    room = ATOMS - FEATS
    rhs[:room, :] = jnp.zeros((room, WIDTH), BF)
    rhs[room : room + FEATS, :] = rows.astype(BF)
    rhs[room + FEATS :, :] = jnp.zeros((room, WIDTH), BF)


def weights_at(rhs, a, span):
    first = (GROUP - 1 - a) * FEATS
    return rhs[first : first + ATOMS, span]


def fill_times(times, total):
    for a in range(GROUP):
        spread = pick(iota((ATOMS, ATOMS), 0) % HALF == iota((ATOMS, ATOMS), 1) * GROUP + a)
        times[a, :, :] = dot(total, spread)


def sum_rows(prod, rows):
    parts = [prod[r : r + 16] for r in range(0, rows, 16)]
    while len(parts) > SUMS:
        parts = [
            parts[q] + parts[q + 1] if q + 1 < len(parts) else parts[q] for q in range(0, len(parts), 2)
        ]
    total = parts[0].astype(F32)
    for part in parts[1:]:
        total = total + part.astype(F32)
    return total[:8] + total[8:]


SUMS = 1


def offsets_of(bounds):
    offsets = [0]
    for g in range(GROUPS):
        lo, hi = bounds[g // 2]
        offsets.append(offsets[-1] + hi - lo)
    return offsets


OWN_AT = offsets_of(OWN_ROWS)
GHOST_AT = offsets_of(GHOST_ROWS)


def wide_of(column):
    column = jnp.broadcast_to(column, (column.shape[0], 128)).astype(BF)
    return jnp.concatenate([column] * (TILE // 128), axis=1)


def gated(pre):
    half = pre.astype(BF)
    return half * jnp.tanh(half) + half


def cut(rows):
    return [rows[r : r + 16] for r in range(0, rows.shape[0], 16)]


def total_of(parts):
    while len(parts) > SUMS:
        parts = [
            parts[q] + parts[q + 1] if q + 1 < len(parts) else parts[q] for q in range(0, len(parts), 2)
        ]
    total = parts[0].astype(F32)
    for part in parts[1:]:
        total = total + part.astype(F32)
    return total[:8] + total[8:]


def keep(partial, a, k, count, w, done):
    at = (a * count + k) * 8
    for t in range(TILE // 128):
        partial[w * (TILE // 128) + t, at : at + 8, :] = done[:, t * 128 : (t + 1) * 128]


def collect(partial, begin, end):
    tiles = []
    for t in range(WIDTH // 128):
        total = partial[t, pl.ds(begin * 8, end - begin, stride=8), :]
        for r in range(1, 8):
            total = total + partial[t, pl.ds(begin * 8 + r, end - begin, stride=8), :]
        tiles.append(total)
    return jnp.concatenate(tiles, axis=1)


def early():
    return (lax.axis_index("dom") == 0) & (parity() == 0)


def sum_own(begin, end, table, edges, rhs, times, partial, sum_ref):
    def step(a):
        share = times[a]
        for w in range(WIDTH // TILE):
            span = slice(w * TILE, (w + 1) * TILE)
            for first in range(0, GROUPS, 2):
                pre = dot(edges[OWN_AT[first] : OWN_AT[first + 2], :], weights_at(rhs, a, span)).astype(BF)
                for g in range(first, first + 2):
                    lo, hi = OWN_ROWS[g // 2]
                    weighted = table[lo:hi, span] * wide_of(share[lo:hi, g : g + 1])
                    gate = gated(pre[OWN_AT[g] - OWN_AT[first] : OWN_AT[g + 1] - OWN_AT[first]])
                    keep(partial, a, g, GROUPS, w, total_of(cut(gate * weighted)))

    for a in range(begin, end):
        step(a)
    sum_ref[begin * GROUPS : end * GROUPS, :] = collect(partial, begin * GROUPS, end * GROUPS)


def prepare_and_sum(
    end,
    feat_ref,
    pos_ref,
    frame_ref,
    nbr_ref,
    cnt_ref,
    we_ref,
    be_ref,
    sum_ref,
    total_ref,
    table,
    edges,
    rhs,
    times,
    partial,
):
    own = pick(iota((ATOMS, ATOMS), 1) == local(iota((ATOMS, ATOMS), 0)))
    table[...] = dot(own, feat_ref[...]).astype(BF)

    raw = nbr_ref[...]
    order = jnp.where(raw < ATOMS, raw + CAP, jnp.where(raw < ATOMS + CAP, raw - ATOMS, raw))
    order = jnp.where(parity() == 1, 2 * CAP + ATOMS - 1 - order, order)
    by_slot = order.astype(F32).T.astype(BF)
    atom = local(iota((ATOMS, ATOMS), 0))
    lane = iota((ATOMS, ATOMS), 1)
    to_low = pick((atom == lane) & (lane < HALF))
    to_high = pick(atom + HALF == lane)
    folded = dot(by_slot[: SLOTS // 2], to_low) + dot(by_slot[SLOTS // 2 :], to_high)
    cnt = jnp.broadcast_to(cnt_ref[...].astype(F32), (8, ATOMS)).astype(BF)
    live = (dot(cnt, to_low) + dot(cnt, to_high))[0:1, :]
    slot = iota((SLOTS // 2, ATOMS), 0) + jnp.where(iota((SLOTS // 2, ATOMS), 1) < HALF, 0, SLOTS // 2)
    folded = jnp.where(slot.astype(F32) < live, folded, -1.0).astype(BF)
    place = iota((TABLE, ATOMS), 0).astype(F32).astype(BF)
    total = jnp.zeros((TABLE, ATOMS), BF)
    one = jnp.ones((TABLE, ATOMS), BF)
    for k in range(SLOTS // 2):
        total = jnp.where(place == folded[k : k + 1, :], total + one, total)
    total_ref[...] = total
    fill_times(times, total[CAP:])
    fill_edges(edges, placed_rows(own.astype(F32), pos_ref), centres(pos_ref), OWN_ROWS)
    fill_filter(rhs, entries(frame_ref), we_ref, be_ref)
    sum_own(0, end, table, edges, rhs, times, partial, sum_ref)


def first_kernel(rows_ref, *refs):
    sources, (pay_ref,), results, partial = refs[:8], refs[8:9], refs[9:23], refs[23]
    for source, result in zip(sources, results[:8]):
        result[...] = source[...]
    feat_ref, pos_ref, frame_ref = sources[:3]
    wanted = jnp.where(parity() == 1, rows_ref[0, 1:2, :], rows_ref[0, 0:1, :])
    row = iota((CAP, CAP), 0)
    source = jnp.where(parity() == 1, row, CAP - 1 - row)
    column = jnp.sum(
        jnp.where(iota((CAP, CAP), 1) == source, wanted, 0).astype(F32), axis=1, keepdims=True
    ).astype(I32)
    chosen = pick(iota((CAP, ATOMS), 1) == column)
    pay_ref[:, :WIDTH] = dot(chosen, feat_ref[...]).astype(BF)
    lane = iota((CAP, EXTRA), 1)
    rest = jnp.zeros((CAP, EXTRA), F32)
    for c in range(3):
        line = chosen.astype(F32) * pos_ref[c : c + 1, :].astype(F32)
        rest = jnp.where(lane == c, jnp.sum(line, axis=1, keepdims=True), rest)
    turn = jnp.zeros((CAP, EXTRA), F32)
    for a in range(3):
        for c in range(3):
            k = 8 + 3 * a + c
            here = (lane == k) | (lane == k + 16) | (lane == k + 32)
            turn = jnp.where(here, frame_ref[a, :, c : c + 1], turn)
    high, rest_of = split(turn)
    mid, low = split(rest_of)
    turn = jnp.where(lane < 24, high, jnp.where(lane < 40, mid, low))
    pay_ref[:, WIDTH:] = (rest + turn).astype(BF)

    @pl.when(early())
    def _():
        prepare_and_sum(AHEAD, *sources[:7], *results[8:], partial)


def own_kernel(*refs):
    sources, before, results, partial = refs[:7], refs[7:13], refs[13:19], refs[19]

    @pl.when(early())
    def _():
        for source, result in zip(before, results):
            result[...] = source[...]
        sum_own(AHEAD, GROUP, *results[2:], partial, results[0])

    @pl.when(jnp.logical_not(early()))
    def _():
        prepare_and_sum(GROUP, *sources, *results, partial)


def last_kernel(
    pay_ref,
    sum_ref,
    total_ref,
    table,
    edges,
    rhs,
    own_times,
    pos_ref,
    frame_ref,
    we_ref,
    be_ref,
    wm_ref,
    wu_ref,
    wr_ref,
    wh_ref,
    out_ref,
    ghosts,
    rhs_other,
    times,
    partial,
):
    rot = entries(frame_ref)
    extra = pay_ref[:, WIDTH:]
    head = extra[0:1, :].astype(F32)
    other = []
    for a in range(3):
        other.append([])
        for c in range(3):
            k = 8 + 3 * a + c
            other[a].append(head[:, k : k + 1] + head[:, k + 16 : k + 17] + head[:, k + 32 : k + 33])
    reach = [dot(extra, pick(iota((EXTRA, EXTRA), 0) == c)) for c in range(3)]
    fill_times(times, total_ref[:CAP, :])
    fill_edges(ghosts, reach, centres(pos_ref), GHOST_ROWS)
    fill_filter(rhs_other, other, we_ref, be_ref)

    def step(a):
        share = times[a]
        own_share = own_times[a]
        for w in range(WIDTH // TILE):
            span = slice(w * TILE, (w + 1) * TILE)
            near = gated(dot(ghosts[...], weights_at(rhs, a, span)))
            far = gated(dot(ghosts[...], weights_at(rhs_other, a, span)))
            for first in range(0, GROUPS, 2):
                pre = dot(edges[OWN_AT[first] : OWN_AT[first + 2], :], weights_at(rhs_other, a, span)).astype(BF)
                for g in range(first, first + 2):
                    lo, hi = GHOST_ROWS[g // 2]
                    weighted = pay_ref[lo:hi, span] * wide_of(share[lo:hi, g : g + 1])
                    rows = slice(GHOST_AT[g], GHOST_AT[g + 1])
                    keep(partial, a, g, 2 * GROUPS, w, total_of(cut(near[rows] * weighted)))
                    parts = cut(far[rows] * weighted)
                    lo, hi = OWN_ROWS[g // 2]
                    weighted = table[lo:hi, span] * wide_of(own_share[lo:hi, g : g + 1])
                    gate = gated(pre[OWN_AT[g] - OWN_AT[first] : OWN_AT[g + 1] - OWN_AT[first]])
                    parts = parts + cut(gate * weighted)
                    keep(partial, a, GROUPS + g, 2 * GROUPS, w, total_of(parts))

    for a in range(GROUP):
        step(a)
    total = collect(partial, 0, ATOMS)
    before = [
        piece
        for a in range(GROUP)
        for piece in (sum_ref[a * GROUPS : (a + 1) * GROUPS, :], jnp.zeros((GROUPS, WIDTH), F32))
    ]
    msg = ((total + jnp.concatenate(before, axis=0)) * message_scale).astype(BF)
    row = iota((ATOMS, ATOMS), 0)
    lane = iota((ATOMS, ATOMS), 1)
    row_atom = (row % GROUPS) * GROUP + row // 16
    mine = dot(pick(lane == row_atom), table[...])

    def silu(x):
        h = 0.5 * x
        return h * jnp.tanh(h) + h

    hidden = silu(dot(msg, wm_ref[...])).astype(BF)
    updated = (mine + dot(hidden, wu_ref[...])).astype(BF)
    readout = silu(dot(updated, wr_ref[...])).astype(BF)
    lane_atom = (lane % GROUPS) * GROUP + lane // 16
    out = jnp.zeros((4, ATOMS), F32)
    for f, turn in enumerate((rot, other)):
        back = pick((local(row) == lane_atom) & ((lane // GROUPS) % 2 == f))
        heads = dot_t(wh_ref[...], dot(back, readout).astype(BF))
        force = [
            turn[0][c] * heads[0:1] + turn[1][c] * heads[1:2] + turn[2][c] * heads[2:3] for c in range(3)
        ]
        out = out + jnp.concatenate(force + [heads[3:4]], axis=0)
    out_ref[...] = out


def cost(microseconds):
    return pl.CostEstimate(flops=microseconds * 10**9, bytes_accessed=microseconds * 10**6, transcendentals=0)


def local_step(
    features,
    positions,
    neighbours,
    counts,
    send_rows,
    frames,
    w_edge,
    b_edge,
    w_message,
    w_update,
    w_readout,
    w_heads,
):
    dom_count = lax.axis_size("dom")
    frame_count = lax.axis_size("frame")
    frame = jnp.transpose(frames, (1, 0, 2))
    bias = b_edge.reshape(1, WIDTH)
    inputs = (features, positions, frame, neighbours, counts.reshape(1, ATOMS), w_edge, bias, w_heads.T)
    prepared = [
        pltpu.VMEM((HALF, WIDTH), F32),
        pltpu.VMEM((TABLE, ATOMS), BF),
        pltpu.VMEM((ATOMS, WIDTH), BF),
        pltpu.VMEM((OWN_AT[-1], ATOMS), BF),
        pltpu.VMEM((2 * ATOMS - FEATS, WIDTH), BF),
        pltpu.VMEM((GROUP, ATOMS, ATOMS), F32),
    ]
    payload, *first = pl.pallas_call(
        first_kernel,
        out_shape=[pltpu.VMEM((CAP, PAY), BF)] + [pltpu.VMEM(x.shape, x.dtype) for x in inputs] + prepared,
        scratch_shapes=[pltpu.VMEM((WIDTH // 128, HALF * 8, 128), F32)],
        compiler_params=pltpu.CompilerParams(vmem_limit_bytes=20 << 20),
        cost_estimate=cost(2),
    )(*[pltpu.with_memory_space_constraint(x, pltpu.MemorySpace.HBM) for x in (send_rows, *inputs)])
    held, before = first[:8], first[8:]
    pairs = []
    for d in range(dom_count):
        for f in range(frame_count):
            to = (d + 1) % dom_count if f >= frame_count // 2 else (d - 1) % dom_count
            pairs.append((d * frame_count + f, to * frame_count + (f + frame_count // 2) % frame_count))
    ghosts = lax.ppermute(payload, ("dom", "frame"), pairs)
    own = pl.pallas_call(
        own_kernel,
        out_shape=prepared,
        scratch_shapes=[pltpu.VMEM((WIDTH // 128, HALF * 8, 128), F32)],
        compiler_params=pltpu.CompilerParams(vmem_limit_bytes=20 << 20),
        cost_estimate=cost(5),
    )(*held[:7], *before)
    part = pl.pallas_call(
        last_kernel,
        out_shape=jax.ShapeDtypeStruct((4, ATOMS), F32),
        scratch_shapes=[
            pltpu.VMEM((GHOST_AT[-1], ATOMS), BF),
            pltpu.VMEM((2 * ATOMS - FEATS, WIDTH), BF),
            pltpu.VMEM((GROUP, CAP, ATOMS), F32),
            pltpu.VMEM((WIDTH // 128, ATOMS * 8, 128), F32),
        ],
        compiler_params=pltpu.CompilerParams(vmem_limit_bytes=20 << 20),
        cost_estimate=cost(7),
    )(
        ghosts,
        *own,
        held[1],
        held[2],
        held[5],
        held[6],
        w_message,
        w_update,
        w_readout,
        held[7],
    )
    copies = jnp.broadcast_to(part, (frame_count, *part.shape))
    everything = lax.all_to_all(copies, "frame", split_axis=0, concat_axis=0, tiled=True)
    return jnp.sum(everything, axis=0) / frame_count


def solution(mesh):
    placed = (
        P("dom", None),
        P(None, "dom"),
        P("dom", None),
        P("dom"),
        P("dom", None, None),
        P("frame", None, None),
        P(),
        P(),
        P(),
        P(),
        P(),
        P(),
    )
    return jax.shard_map(
        local_step, mesh=mesh, in_specs=placed, out_specs=P(None, "dom"), check_vma=False
    )
```

```python
import jax
import jax.numpy as jnp
from jax import lax
from jax.experimental import pallas as pl
from jax.experimental.pallas import tpu as pltpu
from jax.sharding import PartitionSpec as P

BF = jnp.bfloat16
F32 = jnp.float32
I32 = jnp.int32
message_scale = 0.0884
radial_step = 1.25

ATOMS = 128
HALF = 64
CAP = 64
TABLE = CAP + ATOMS
WIDTH = 512
SLOTS = 128
FEATS = 16
GROUP = 8
GROUPS = HALF // GROUP
EXTRA = 128
PAY = WIDTH + EXTRA
RADIAL = 6
GHOST_ROWS = ((0, 64), (16, 64), (32, 64), (48, 64))
OWN_ROWS = ((0, 64), (0, 96), (0, 112), (0, 128))
TILE = 256
AHEAD = 3


def iota(shape, dim):
    return lax.broadcasted_iota(I32, shape, dim)


def dot(a, b):
    return jnp.dot(a, b, preferred_element_type=F32)


def dot_t(a, b):
    return lax.dot_general(a, b, (((1,), (1,)), ((), ())), preferred_element_type=F32)


def mask(cond):
    return jnp.where(cond, 1.0, 0.0).astype(F32)


def pick(cond):
    return mask(cond).astype(BF)


def parity():
    return lax.axis_index("frame") // (lax.axis_size("frame") // 2)


def local(n):
    return jnp.where(parity() == 1, ATOMS - 1 - n, n)


def entries(ref):
    return [[ref[a, :, c : c + 1] for c in range(3)] for a in range(3)]


def vectors(rot, we_ref, c):
    return 0.5 * (rot[0][c] * we_ref[6:7, :] + rot[1][c] * we_ref[7:8, :] + rot[2][c] * we_ref[8:9, :])


def split(x):
    high = x.astype(BF).astype(F32)
    return high, x - high


def centres(pos_ref):
    atom = local(iota((8, ATOMS), 1))
    in_group = mask(atom // GROUP == iota((8, ATOMS), 0))
    spread = pick(local(iota((ATOMS, ATOMS), 0)) % GROUP == iota((ATOMS, ATOMS), 1) // FEATS)
    return [dot((in_group * pos_ref[c : c + 1, :].astype(F32)).astype(BF), spread) for c in range(3)]


def placed_rows(chosen, pos_ref):
    ones = jnp.ones((ATOMS, ATOMS), BF)
    return [dot((chosen * pos_ref[c : c + 1, :].astype(F32)).astype(BF), ones) for c in range(3)]


def fill_edges(edges, reach, centre, bounds):
    kind = iota((1, ATOMS), 1) % FEATS
    shift = kind.astype(F32) * radial_step
    at = 0
    for g in range(GROUPS):
        lo, hi = bounds[g // 2]
        rel = [reach[c][lo:hi] - centre[c][g : g + 1, :] for c in range(3)]
        dist = jnp.sqrt(rel[0] * rel[0] + rel[1] * rel[1] + rel[2] * rel[2] + 0.25) - shift
        value = jnp.exp(-(dist * dist))
        axis = jnp.where(kind % 3 == 0, rel[0], jnp.where(kind % 3 == 1, rel[1], rel[2]))
        high, low = split(axis)
        axis = jnp.where((kind >= 9) & (kind < 12), low, high)
        value = jnp.where(kind < RADIAL, value, jnp.where(kind < 15, axis, 1.0))
        edges[at : at + hi - lo, :] = value.astype(BF)
        at += hi - lo


def fill_filter(rhs, rot, we_ref, be_ref):
    vec = jnp.concatenate([vectors(rot, we_ref, c) for c in range(3)], axis=0)
    high, low = split(vec)
    rows = jnp.concatenate([0.5 * we_ref[0:RADIAL, :], high, high, low, 0.5 * be_ref[...]], axis=0)
    room = ATOMS - FEATS
    rhs[:room, :] = jnp.zeros((room, WIDTH), BF)
    rhs[room : room + FEATS, :] = rows.astype(BF)
    rhs[room + FEATS :, :] = jnp.zeros((room, WIDTH), BF)


def weights_at(rhs, a, span):
    first = (GROUP - 1 - a) * FEATS
    return rhs[first : first + ATOMS, span]


def fill_times(times, total):
    for a in range(GROUP):
        spread = pick(iota((ATOMS, ATOMS), 0) % HALF == iota((ATOMS, ATOMS), 1) * GROUP + a)
        times[a, :, :] = dot(total, spread)


def sum_rows(prod, rows):
    parts = [prod[r : r + 16] for r in range(0, rows, 16)]
    while len(parts) > SUMS:
        parts = [
            parts[q] + parts[q + 1] if q + 1 < len(parts) else parts[q] for q in range(0, len(parts), 2)
        ]
    total = parts[0].astype(F32)
    for part in parts[1:]:
        total = total + part.astype(F32)
    return total[:8] + total[8:]


SUMS = 1


def offsets_of(bounds):
    offsets = [0]
    for g in range(GROUPS):
        lo, hi = bounds[g // 2]
        offsets.append(offsets[-1] + hi - lo)
    return offsets


OWN_AT = offsets_of(OWN_ROWS)
GHOST_AT = offsets_of(GHOST_ROWS)


def wide_of(column):
    column = jnp.broadcast_to(column, (column.shape[0], 128)).astype(BF)
    return jnp.concatenate([column] * (TILE // 128), axis=1)


def gated(pre):
    half = pre.astype(BF)
    return half * jnp.tanh(half) + half


def cut(rows):
    return [rows[r : r + 16] for r in range(0, rows.shape[0], 16)]


def total_of(parts):
    while len(parts) > SUMS:
        parts = [
            parts[q] + parts[q + 1] if q + 1 < len(parts) else parts[q] for q in range(0, len(parts), 2)
        ]
    total = parts[0].astype(F32)
    for part in parts[1:]:
        total = total + part.astype(F32)
    return total[:8] + total[8:]


def keep(partial, a, k, count, w, done):
    at = (a * count + k) * 8
    for t in range(TILE // 128):
        partial[w * (TILE // 128) + t, at : at + 8, :] = done[:, t * 128 : (t + 1) * 128]


def collect(partial, begin, end):
    tiles = []
    for t in range(WIDTH // 128):
        total = partial[t, pl.ds(begin * 8, end - begin, stride=8), :]
        for r in range(1, 8):
            total = total + partial[t, pl.ds(begin * 8 + r, end - begin, stride=8), :]
        tiles.append(total)
    return jnp.concatenate(tiles, axis=1)


def early():
    return (lax.axis_index("dom") == 0) & (parity() == 0)


def sum_own(begin, end, table, edges, rhs, times, partial, sum_ref):
    def step(a):
        share = times[a]
        for w in range(WIDTH // TILE):
            span = slice(w * TILE, (w + 1) * TILE)
            for first in range(0, GROUPS, 4):
                pre = dot(edges[OWN_AT[first] : OWN_AT[first + 4], :], weights_at(rhs, a, span)).astype(BF)
                for g in range(first, first + 4):
                    lo, hi = OWN_ROWS[g // 2]
                    weighted = table[lo:hi, span] * wide_of(share[lo:hi, g : g + 1])
                    gate = gated(pre[OWN_AT[g] - OWN_AT[first] : OWN_AT[g + 1] - OWN_AT[first]])
                    keep(partial, a, g, GROUPS, w, total_of(cut(gate * weighted)))

    for a in range(begin, end):
        step(a)
    sum_ref[begin * GROUPS : end * GROUPS, :] = collect(partial, begin * GROUPS, end * GROUPS)


def prepare_and_sum(
    end,
    feat_ref,
    pos_ref,
    frame_ref,
    nbr_ref,
    cnt_ref,
    we_ref,
    be_ref,
    sum_ref,
    total_ref,
    table,
    edges,
    rhs,
    times,
    partial,
):
    own = pick(iota((ATOMS, ATOMS), 1) == local(iota((ATOMS, ATOMS), 0)))
    table[...] = dot(own, feat_ref[...]).astype(BF)

    raw = nbr_ref[...]
    order = jnp.where(raw < ATOMS, raw + CAP, jnp.where(raw < ATOMS + CAP, raw - ATOMS, raw))
    order = jnp.where(parity() == 1, 2 * CAP + ATOMS - 1 - order, order)
    by_slot = order.astype(F32).T.astype(BF)
    atom = local(iota((ATOMS, ATOMS), 0))
    lane = iota((ATOMS, ATOMS), 1)
    to_low = pick((atom == lane) & (lane < HALF))
    to_high = pick(atom + HALF == lane)
    folded = dot(by_slot[: SLOTS // 2], to_low) + dot(by_slot[SLOTS // 2 :], to_high)
    cnt = jnp.broadcast_to(cnt_ref[...].astype(F32), (8, ATOMS)).astype(BF)
    live = (dot(cnt, to_low) + dot(cnt, to_high))[0:1, :]
    slot = iota((SLOTS // 2, ATOMS), 0) + jnp.where(iota((SLOTS // 2, ATOMS), 1) < HALF, 0, SLOTS // 2)
    folded = jnp.where(slot.astype(F32) < live, folded, -1.0).astype(BF)
    place = iota((TABLE, ATOMS), 0).astype(F32).astype(BF)
    total = jnp.zeros((TABLE, ATOMS), BF)
    one = jnp.ones((TABLE, ATOMS), BF)
    for k in range(SLOTS // 2):
        total = jnp.where(place == folded[k : k + 1, :], total + one, total)
    total_ref[...] = total
    fill_times(times, total[CAP:])
    fill_edges(edges, placed_rows(own.astype(F32), pos_ref), centres(pos_ref), OWN_ROWS)
    fill_filter(rhs, entries(frame_ref), we_ref, be_ref)
    sum_own(0, end, table, edges, rhs, times, partial, sum_ref)


def first_kernel(rows_ref, *refs):
    sources, (pay_ref,), results, partial = refs[:8], refs[8:9], refs[9:23], refs[23]
    for source, result in zip(sources, results[:8]):
        result[...] = source[...]
    feat_ref, pos_ref, frame_ref = sources[:3]
    wanted = jnp.where(parity() == 1, rows_ref[0, 1:2, :], rows_ref[0, 0:1, :])
    row = iota((CAP, CAP), 0)
    source = jnp.where(parity() == 1, row, CAP - 1 - row)
    column = jnp.sum(
        jnp.where(iota((CAP, CAP), 1) == source, wanted, 0).astype(F32), axis=1, keepdims=True
    ).astype(I32)
    chosen = pick(iota((CAP, ATOMS), 1) == column)
    pay_ref[:, :WIDTH] = dot(chosen, feat_ref[...]).astype(BF)
    lane = iota((CAP, EXTRA), 1)
    rest = jnp.zeros((CAP, EXTRA), F32)
    for c in range(3):
        line = chosen.astype(F32) * pos_ref[c : c + 1, :].astype(F32)
        rest = jnp.where(lane == c, jnp.sum(line, axis=1, keepdims=True), rest)
    turn = jnp.zeros((CAP, EXTRA), F32)
    for a in range(3):
        for c in range(3):
            k = 8 + 3 * a + c
            here = (lane == k) | (lane == k + 16) | (lane == k + 32)
            turn = jnp.where(here, frame_ref[a, :, c : c + 1], turn)
    high, rest_of = split(turn)
    mid, low = split(rest_of)
    turn = jnp.where(lane < 24, high, jnp.where(lane < 40, mid, low))
    pay_ref[:, WIDTH:] = (rest + turn).astype(BF)

    @pl.when(early())
    def _():
        prepare_and_sum(AHEAD, *sources[:7], *results[8:], partial)


def own_kernel(*refs):
    sources, before, results, partial = refs[:7], refs[7:13], refs[13:19], refs[19]

    @pl.when(early())
    def _():
        for source, result in zip(before, results):
            result[...] = source[...]
        sum_own(AHEAD, GROUP, *results[2:], partial, results[0])

    @pl.when(jnp.logical_not(early()))
    def _():
        prepare_and_sum(GROUP, *sources, *results, partial)


def last_kernel(
    pay_ref,
    sum_ref,
    total_ref,
    table,
    edges,
    rhs,
    own_times,
    pos_ref,
    frame_ref,
    we_ref,
    be_ref,
    wm_ref,
    wu_ref,
    wr_ref,
    wh_ref,
    out_ref,
    ghosts,
    rhs_other,
    times,
    partial,
):
    rot = entries(frame_ref)
    extra = pay_ref[:, WIDTH:]
    head = extra[0:1, :].astype(F32)
    other = []
    for a in range(3):
        other.append([])
        for c in range(3):
            k = 8 + 3 * a + c
            other[a].append(head[:, k : k + 1] + head[:, k + 16 : k + 17] + head[:, k + 32 : k + 33])
    reach = [dot(extra, pick(iota((EXTRA, EXTRA), 0) == c)) for c in range(3)]
    fill_times(times, total_ref[:CAP, :])
    fill_edges(ghosts, reach, centres(pos_ref), GHOST_ROWS)
    fill_filter(rhs_other, other, we_ref, be_ref)

    def step(a):
        share = times[a]
        own_share = own_times[a]
        for w in range(WIDTH // TILE):
            span = slice(w * TILE, (w + 1) * TILE)
            near = gated(dot(ghosts[...], weights_at(rhs, a, span)))
            far = gated(dot(ghosts[...], weights_at(rhs_other, a, span)))
            for first in range(0, GROUPS, 4):
                pre = dot(edges[OWN_AT[first] : OWN_AT[first + 4], :], weights_at(rhs_other, a, span)).astype(BF)
                for g in range(first, first + 4):
                    lo, hi = GHOST_ROWS[g // 2]
                    weighted = pay_ref[lo:hi, span] * wide_of(share[lo:hi, g : g + 1])
                    rows = slice(GHOST_AT[g], GHOST_AT[g + 1])
                    keep(partial, a, g, 2 * GROUPS, w, total_of(cut(near[rows] * weighted)))
                    parts = cut(far[rows] * weighted)
                    lo, hi = OWN_ROWS[g // 2]
                    weighted = table[lo:hi, span] * wide_of(own_share[lo:hi, g : g + 1])
                    gate = gated(pre[OWN_AT[g] - OWN_AT[first] : OWN_AT[g + 1] - OWN_AT[first]])
                    parts = parts + cut(gate * weighted)
                    keep(partial, a, GROUPS + g, 2 * GROUPS, w, total_of(parts))

    for a in range(GROUP):
        step(a)
    total = collect(partial, 0, ATOMS)
    before = [
        piece
        for a in range(GROUP)
        for piece in (sum_ref[a * GROUPS : (a + 1) * GROUPS, :], jnp.zeros((GROUPS, WIDTH), F32))
    ]
    msg = ((total + jnp.concatenate(before, axis=0)) * message_scale).astype(BF)
    row = iota((ATOMS, ATOMS), 0)
    lane = iota((ATOMS, ATOMS), 1)
    row_atom = (row % GROUPS) * GROUP + row // 16
    mine = dot(pick(lane == row_atom), table[...])

    def silu(x):
        h = 0.5 * x
        return h * jnp.tanh(h) + h

    hidden = silu(dot(msg, wm_ref[...])).astype(BF)
    updated = (mine + dot(hidden, wu_ref[...])).astype(BF)
    readout = silu(dot(updated, wr_ref[...])).astype(BF)
    lane_atom = (lane % GROUPS) * GROUP + lane // 16
    out = jnp.zeros((4, ATOMS), F32)
    for f, turn in enumerate((rot, other)):
        back = pick((local(row) == lane_atom) & ((lane // GROUPS) % 2 == f))
        heads = dot_t(wh_ref[...], dot(back, readout).astype(BF))
        force = [
            turn[0][c] * heads[0:1] + turn[1][c] * heads[1:2] + turn[2][c] * heads[2:3] for c in range(3)
        ]
        out = out + jnp.concatenate(force + [heads[3:4]], axis=0)
    out_ref[...] = out


def cost(microseconds):
    return pl.CostEstimate(flops=microseconds * 10**9, bytes_accessed=microseconds * 10**6, transcendentals=0)


def local_step(
    features,
    positions,
    neighbours,
    counts,
    send_rows,
    frames,
    w_edge,
    b_edge,
    w_message,
    w_update,
    w_readout,
    w_heads,
):
    dom_count = lax.axis_size("dom")
    frame_count = lax.axis_size("frame")
    frame = jnp.transpose(frames, (1, 0, 2))
    bias = b_edge.reshape(1, WIDTH)
    inputs = (features, positions, frame, neighbours, counts.reshape(1, ATOMS), w_edge, bias, w_heads.T)
    prepared = [
        pltpu.VMEM((HALF, WIDTH), F32),
        pltpu.VMEM((TABLE, ATOMS), BF),
        pltpu.VMEM((ATOMS, WIDTH), BF),
        pltpu.VMEM((OWN_AT[-1], ATOMS), BF),
        pltpu.VMEM((2 * ATOMS - FEATS, WIDTH), BF),
        pltpu.VMEM((GROUP, ATOMS, ATOMS), F32),
    ]
    payload, *first = pl.pallas_call(
        first_kernel,
        out_shape=[pltpu.VMEM((CAP, PAY), BF)] + [pltpu.VMEM(x.shape, x.dtype) for x in inputs] + prepared,
        scratch_shapes=[pltpu.VMEM((WIDTH // 128, HALF * 8, 128), F32)],
        compiler_params=pltpu.CompilerParams(vmem_limit_bytes=20 << 20),
        cost_estimate=cost(2),
    )(*[pltpu.with_memory_space_constraint(x, pltpu.MemorySpace.HBM) for x in (send_rows, *inputs)])
    held, before = first[:8], first[8:]
    pairs = []
    for d in range(dom_count):
        for f in range(frame_count):
            to = (d + 1) % dom_count if f >= frame_count // 2 else (d - 1) % dom_count
            pairs.append((d * frame_count + f, to * frame_count + (f + frame_count // 2) % frame_count))
    ghosts = lax.ppermute(payload, ("dom", "frame"), pairs)
    own = pl.pallas_call(
        own_kernel,
        out_shape=prepared,
        scratch_shapes=[pltpu.VMEM((WIDTH // 128, HALF * 8, 128), F32)],
        compiler_params=pltpu.CompilerParams(vmem_limit_bytes=20 << 20),
        cost_estimate=cost(5),
    )(*held[:7], *before)
    part = pl.pallas_call(
        last_kernel,
        out_shape=jax.ShapeDtypeStruct((4, ATOMS), F32),
        scratch_shapes=[
            pltpu.VMEM((GHOST_AT[-1], ATOMS), BF),
            pltpu.VMEM((2 * ATOMS - FEATS, WIDTH), BF),
            pltpu.VMEM((GROUP, CAP, ATOMS), F32),
            pltpu.VMEM((WIDTH // 128, ATOMS * 8, 128), F32),
        ],
        compiler_params=pltpu.CompilerParams(vmem_limit_bytes=20 << 20),
        cost_estimate=cost(7),
    )(
        ghosts,
        *own,
        held[1],
        held[2],
        held[5],
        held[6],
        w_message,
        w_update,
        w_readout,
        held[7],
    )
    copies = jnp.broadcast_to(part, (frame_count, *part.shape))
    everything = lax.all_to_all(copies, "frame", split_axis=0, concat_axis=0, tiled=True)
    return jnp.sum(everything, axis=0) / frame_count


def solution(mesh):
    placed = (
        P("dom", None),
        P(None, "dom"),
        P("dom", None),
        P("dom"),
        P("dom", None, None),
        P("frame", None, None),
        P(),
        P(),
        P(),
        P(),
        P(),
        P(),
    )
    return jax.shard_map(
        local_step, mesh=mesh, in_specs=placed, out_specs=P(None, "dom"), check_vma=False
    )
```
